256 devices in a mesh: feat: 64 (over x, y_hi, z), tgt: 4 (over y_lo, core).
Axes of the slice: x: 4, y: 4 (y_hi: 2, y_lo: 2; y = y_hi * 2 + y_lo), z: 8, core: 2. Of those that a mesh axis runs over, the one named last changes fastest.
Arguments:
- sources: bfloat16 [4, 128, 2304], P('tgt'), may hold values from -6 to 6
- targets: bfloat16 [4, 128, 2304], P('tgt', 'feat'), may hold values from -6 to 6
- enc_weight: bfloat16 [4, 2304, 16384], P('tgt', None, 'feat'), may hold values from -0.125 to 0.125
- enc_bias: float32 [4, 16384], P('tgt', 'feat'), may hold values from -5 to 5
- dec_weight: bfloat16 [4, 4, 16384, 2304], P('tgt', None, 'feat'), may hold values from -0.046875 to 0.046875
- pair_mask: int32 [4, 4], replicated, may hold values from 0 to 1, as said below
Outputs:
- error: bfloat16 [4, 128, 2304], P('tgt', 'feat')
- latent_grad: bfloat16 [4, 128, 16384], P('tgt', None, 'feat')
The draws below stay inside these ranges and needn't reach their ends.
Inputs may be any that keep to these rules, and one draw needn't show every extreme that they name: pair_mask[t, s] is 0 wherever s > t and 1 wherever s == t.
All inputs are finite; a program needn't handle non-finite values.
Results may differ from the reference program's by a relative error of at most 0.0055.
Values may be sent and summed in bfloat16 or wider, within the bound.
No kernel may reach another device: no remote copies, remote signals or barrier semaphores. Data moves between devices by JAX's collectives and lax.ppermute only.
A program may use at most 64 MiB of HBM per device.

```python
import jax
import jax.numpy as jnp
from jax import lax

D = 2304
F = 16384
TOK = 128
LAYERS = 4


def draw_pair_mask(key, part):
    picks = jax.random.randint(key, (LAYERS, LAYERS), 0, 4)
    row_ids = lax.broadcasted_iota(jnp.int32, (LAYERS, LAYERS), 0)
    col_ids = lax.broadcasted_iota(jnp.int32, (LAYERS, LAYERS), 1)
    below = jnp.where(picks > 0, 1, 0).astype(jnp.int32)
    return jnp.where(row_ids == col_ids, 1, jnp.where(row_ids > col_ids, below, 0)).astype(jnp.int32)


def block_scale(stream_key, extent, cuts, smallest, top_value):
    factor_of = 1.0
    for dim, parts in cuts:
        draws = jax.random.uniform(jax.random.fold_in(jax.random.fold_in(stream_key, 6), dim), (parts,), jnp.float32, smallest / len(cuts), top_value / len(cuts))
        factor_of = factor_of * jnp.repeat(jnp.exp(draws), extent[dim] // parts).reshape((-1,) + (1,) * (len(extent) - 1 - dim))
    return factor_of


def gaussian(rng, extent, deviation, limit, cuts=(), kind=jnp.bfloat16):
    loudness = block_scale(rng, extent, cuts, -0.22, 0.18) if cuts else 1.0
    result = jax.random.normal(rng, extent, jnp.float32) * deviation * loudness
    return jnp.minimum(jnp.maximum(result, -limit), limit).astype(kind)


def setup_inputs(seed: int = 0) -> dict:
    key_of = jax.random.split(jax.random.key(seed), 7)
    return {
        "sources": gaussian(key_of[0], (LAYERS, TOK, D), 1.0, 6.0, ((0, 4),)),
        "targets": gaussian(key_of[1], (LAYERS, TOK, D), 1.0, 6.0, ((0, 4), (1, 64))),
        "enc_weight": gaussian(key_of[2], (LAYERS, D, F), D ** -0.5, 0.125, ((0, 4), (2, 64))),
        "enc_bias": gaussian(key_of[3], (LAYERS, F), 1.0, 5.0, ((0, 4), (1, 64)), jnp.float32),
        "dec_weight": gaussian(key_of[4], (LAYERS, LAYERS, F, D), F ** -0.5, 0.046875, ((0, 4), (2, 64))),
        "pair_mask": draw_pair_mask(jax.random.fold_in(key_of[6], 71), 0),
    }


def reference(sources, targets, enc_weight, enc_bias, dec_weight, pair_mask):
    latents = []
    for layer in range(LAYERS):
        pre = jnp.dot(sources[layer], enc_weight[layer], preferred_element_type=jnp.float32) + enc_bias[layer]
        latents.append(jnp.maximum(pre, 0.0).astype(jnp.bfloat16))
    errors = []
    for target in range(LAYERS):
        total = jnp.zeros((TOK, D), jnp.float32)
        for source in range(target + 1):
            weight = pair_mask[target, source].astype(jnp.float32)
            total = total + weight * jnp.dot(latents[source], dec_weight[target, source], preferred_element_type=jnp.float32)
        errors.append((total - targets[target].astype(jnp.float32)).astype(jnp.bfloat16))
    grads = []
    for source in range(LAYERS):
        total = jnp.zeros((TOK, F), jnp.float32)
        for target in range(source, LAYERS):
            weight = pair_mask[target, source].astype(jnp.float32)
            term = lax.dot_general(errors[target], dec_weight[target, source], (((1,), (1,)), ((), ())), preferred_element_type=jnp.float32)
            total = total + weight * term
        grads.append(total.astype(jnp.bfloat16))
    return jnp.stack(errors), jnp.stack(grads)
```

```python
import jax
import jax.numpy as jnp
from jax import lax
from jax.sharding import Mesh, PartitionSpec as P

X, YH, ZH, ZL, TG = 4, 2, 4, 2, 4
NEAR = ("x", "yh", "zl")
FEAT = ("x", "yh", "zh", "zl")
DOT = dict(preferred_element_type=jnp.float32)


def per_device(sources, targets, enc_weight, enc_bias, dec_weight, pair_mask):
    tok, width = sources.shape[1], sources.shape[2]
    feats = enc_weight.shape[2]
    owner = lax.axis_index("tgt")
    spot = lax.axis_index(FEAT)
    rows_local = targets.shape[1]
    group = X * YH * ZL
    rows = tok // group
    mask_row = lax.dynamic_index_in_dim(pair_mask, owner, 0, keepdims=False)

    pre = jnp.dot(sources[0], enc_weight[0], **DOT) + enc_bias[0]
    latent = jnp.maximum(pre, 0.0).astype(jnp.bfloat16)
    dec = dec_weight[0]

    def weight(index):
        return lax.dynamic_index_in_dim(mask_row, index, 0, keepdims=False)

    def slab(index):
        return lax.dynamic_index_in_dim(dec, index, 0, keepdims=False)

    got = {}
    for flip in (2, 3, 1):
        pairs = [(s, s ^ flip) for s in range(TG) if s < (s ^ flip)]
        got[flip] = lax.ppermute(latent, "tgt", pairs)
    got[0] = latent
    total = None
    for flip in (0, 1, 2, 3):
        peer = owner ^ flip
        keep = weight(peer).astype(jnp.float32)
        part = keep * jnp.dot(got[flip], slab(peer), **DOT)
        total = part if total is None else total + part

    row_ids = lax.broadcasted_iota(jnp.int32, (tok, rows_local), 0)
    col_ids = lax.broadcasted_iota(jnp.int32, (tok, rows_local), 1)
    place = (row_ids == spot * rows_local + col_ids).astype(jnp.bfloat16)
    total = total - jnp.dot(place, targets[0], **DOT)

    shares = total.astype(jnp.bfloat16).reshape(group, rows, width)
    shares = lax.all_to_all(shares, NEAR, 0, 0, tiled=True)
    near = jnp.sum(shares.astype(jnp.float32), axis=0)
    spread = jnp.broadcast_to(near[None], (ZH, rows, width))
    spread = lax.all_to_all(spread, "zh", 0, 0, tiled=True)
    err = jnp.sum(spread, axis=0).astype(jnp.bfloat16)
    copies = jnp.broadcast_to(err[None], (group, rows, width))
    err_full = lax.all_to_all(copies, NEAR, 0, 0, tiled=True).reshape(tok, width)
    err_local = lax.dynamic_slice_in_dim(err_full, spot * rows_local, rows_local, 0)

    grad = None
    for flip in (2, 3, 1, 0):
        peer = owner ^ flip
        keep = weight(peer).astype(jnp.float32)
        term = keep * lax.dot_general(err_full, slab(peer), (((1,), (1,)), ((), ())), **DOT)
        if flip:
            pairs = [(t, t ^ flip) for t in range(TG) if t > (t ^ flip)]
            term = lax.ppermute(term, "tgt", pairs)
        grad = term if grad is None else grad + term
    return (err_local[None], grad.astype(jnp.bfloat16)[None])


def solution(mesh):
    grid = Mesh(
        mesh.devices.reshape(X, YH, ZH, ZL, TG), ("x", "yh", "zh", "zl", "tgt")
    )
    in_specs = (
        P("tgt", None, None),
        P("tgt", FEAT, None),
        P("tgt", None, FEAT),
        P("tgt", FEAT),
        P("tgt", None, FEAT, None),
        P(),
    )
    out_specs = (P("tgt", FEAT, None), P("tgt", None, FEAT))
    return jax.shard_map(
        per_device, mesh=grid, in_specs=in_specs, out_specs=out_specs, check_vma=False
    )
```

```python
import jax
import jax.numpy as jnp
from jax import lax
from jax.experimental import pallas as pl
from jax.experimental.pallas import tpu as pltpu
from jax.sharding import Mesh, PartitionSpec as P

X, YH, ZH, ZL, TG = 4, 2, 4, 2, 4
NEAR = ("x", "yh", "zl")
FEAT = ("x", "yh", "zh", "zl")
GROUP = X * YH * ZL
DOT = dict(preferred_element_type=jnp.float32)
BF, F32 = jnp.bfloat16, jnp.float32
VMEM = pl.BlockSpec(memory_space=pltpu.VMEM)
ANY = pl.BlockSpec(memory_space=pl.ANY)
SMEM = pl.BlockSpec(memory_space=pltpu.SMEM)
LIMIT = 24 * 1024 * 1024
FLIPS = (1, 2, 3)


def cost(flops, moved):
    return pl.CostEstimate(flops=flops, bytes_accessed=moved, transcendentals=0)


def spot_of():
    index = lax.axis_index("x")
    for name, size in (("yh", YH), ("zh", ZH), ("zl", ZL)):
        index = index * size + lax.axis_index(name)
    return index


def encode_kernel(sources, weight, bias, latent, src, wts, shift, sems):
    chunks = wts.shape[0]
    depth = wts.shape[1]
    last = pltpu.make_async_copy(bias, shift, sems.at[chunks + 1])
    last.start()
    copies = [pltpu.make_async_copy(sources, src, sems.at[chunks])]
    for i in range(chunks):
        part = weight.at[pl.ds(i * depth, depth), :]
        copies.append(pltpu.make_async_copy(part, wts.at[i], sems.at[i]))
    for copy in copies:
        copy.start()
    copies[0].wait()
    total = None
    for i in range(chunks):
        copies[i + 1].wait()
        part = jnp.dot(src[:, pl.ds(i * depth, depth)], wts[i], **DOT)
        total = part if total is None else total + part
    last.wait()
    latent[...] = jnp.maximum(total + shift[...], 0.0).astype(BF)


def load_kernel(dec, held, sem):
    copy = pltpu.make_async_copy(dec, held, sem)
    copy.start()
    copy.wait()


def decode_kernel(mask, l0, l1, l2, l3, targets, dec, out):
    owner = lax.axis_index("tgt")
    base = spot_of() * targets.shape[0]
    tok, width = out.shape
    step = 256
    rows = []
    for flip, ref in enumerate((l0, l1, l2, l3)):
        peer = owner ^ flip
        rows.append((peer, ref[...] * mask[owner, peer].astype(F32).astype(BF)))
    row_ids = lax.broadcasted_iota(jnp.int32, (tok, 1), 0)
    for start in range(0, width, step):
        cols = pl.ds(start, step)
        total = None
        for peer, latent in rows:
            part = jnp.dot(latent, dec[peer, :, cols], **DOT)
            total = part if total is None else total + part
        for r in range(targets.shape[0]):
            own = targets[r : r + 1, cols].astype(F32)
            total = total - jnp.where(row_ids == base + r, own, 0.0)
        out[:, cols] = total.astype(BF)


def gather_sum_kernel(shares, out):
    total = shares[0].astype(F32)
    for i in range(1, shares.shape[0]):
        total = total + shares[i].astype(F32)
    out[...] = total.astype(out.dtype)


def spread_kernel(s0, s1, s2, s3, out):
    total = (s0[...].astype(F32) + s1[...].astype(F32)) + (
        s2[...].astype(F32) + s3[...].astype(F32)
    )
    err = total.astype(BF)
    for i in range(out.shape[0]):
        out[i] = err


def grad_kernel(mask, err, dec, g0, g1, g2, g3):
    owner = lax.axis_index("tgt")
    for flip, ref in ((3, g3), (2, g2), (1, g1), (0, g0)):
        peer = owner ^ flip
        keep = mask[owner, peer].astype(F32)
        term = lax.dot_general(err[...], dec[peer], (((1,), (1,)), ((), ())), **DOT)
        ref[...] = (keep * term).astype(ref.dtype)


def pick_kernel(err, out):
    base = spot_of() * out.shape[0]
    block = pl.multiple_of(base // 16 * 16, 16)
    value = err[pl.ds(block, 16), :].astype(F32)
    row_ids = lax.broadcasted_iota(jnp.int32, (16, 1), 0) + block
    for r in range(out.shape[0]):
        row = jnp.sum(jnp.where(row_ids == base + r, value, 0.0), axis=0, keepdims=True)
        out[r : r + 1, :] = row.astype(out.dtype)


def in_hbm(value):
    return pltpu.with_memory_space_constraint(value, pltpu.HBM)


def call(kernel, outs, specs, flops=0, moved=0, scratch=(), out_spec=VMEM):
    return pl.pallas_call(
        kernel,
        out_shape=outs,
        in_specs=specs,
        out_specs=jax.tree.map(lambda _: out_spec, outs),
        scratch_shapes=scratch,
        cost_estimate=cost(flops, moved),
        compiler_params=pltpu.CompilerParams(vmem_limit_bytes=LIMIT),
    )


def per_device(sources, targets, enc_weight, enc_bias, dec_weight, pair_mask):
    tok, width = sources.shape[1], sources.shape[2]
    feats = enc_weight.shape[2]
    rows_local = targets.shape[1]
    rows = tok // GROUP
    shape = jax.ShapeDtypeStruct

    chunks = 6
    latent = call(
        encode_kernel,
        shape((tok, feats), BF),
        [ANY, ANY, ANY],
        2 * tok * feats * width,
        2 * feats * width,
        scratch=[
            pltpu.VMEM((tok, width), BF),
            pltpu.VMEM((chunks, width // chunks, feats), BF),
            pltpu.VMEM((1, feats), F32),
            pltpu.SemaphoreType.DMA((chunks + 2,)),
        ],
    )(in_hbm(sources[0]), in_hbm(enc_weight[0]), in_hbm(enc_bias))
    dec = call(
        load_kernel,
        shape((TG, feats, width), BF),
        [ANY],
        0,
        2 * TG * feats * width,
        scratch=[pltpu.SemaphoreType.DMA],
        out_spec=ANY,
    )(in_hbm(dec_weight[0]))

    got = [latent]
    for flip in FLIPS:
        pairs = [(s, s ^ flip) for s in range(TG) if s < (s ^ flip)]
        got.append(lax.ppermute(latent, "tgt", pairs))
    flops = 2 * TG * tok * feats * width
    shares = call(
        decode_kernel,
        shape((tok, width), BF),
        [SMEM] + [VMEM] * 6,
        flops,
    )(pair_mask, *got, targets[0], dec)

    shares = shares.reshape(GROUP, rows, width)
    shares = lax.all_to_all(shares, NEAR, 0, 0, tiled=True)
    near = call(gather_sum_kernel, shape((rows, width), BF), [VMEM])(shares)
    parts = [near]
    for flip in FLIPS:
        parts.append(lax.ppermute(near, "zh", [(s, s ^ flip) for s in range(ZH)]))
    copies = call(spread_kernel, shape((GROUP, rows, width), BF), [VMEM] * 4)(*parts)
    err_full = lax.all_to_all(copies, NEAR, 0, 0, tiled=True).reshape(tok, width)

    terms = call(
        grad_kernel,
        [shape((tok, feats), F32)] + [shape((tok, feats), BF)] * 3,
        [SMEM] + [VMEM] * 2,
        flops,
    )(pair_mask, err_full, dec)
    err_local = call(pick_kernel, shape((rows_local, width), BF), [VMEM])(err_full)
    grad = terms[0]
    for flip in (3, 2, 1):
        pairs = [(t, t ^ flip) for t in range(TG) if t > (t ^ flip)]
        grad = grad + lax.ppermute(terms[flip], "tgt", pairs).astype(F32)
    return (err_local[None], grad.astype(BF)[None])


def solution(mesh):
    grid = Mesh(
        mesh.devices.reshape(X, YH, ZH, ZL, TG), ("x", "yh", "zh", "zl", "tgt")
    )
    in_specs = (
        P("tgt", None, None),
        P("tgt", FEAT, None),
        P("tgt", None, FEAT),
        P("tgt", FEAT),
        P("tgt", None, FEAT, None),
        P(),
    )
    out_specs = (P("tgt", FEAT, None), P("tgt", None, FEAT))
    return jax.shard_map(
        per_device, mesh=grid, in_specs=in_specs, out_specs=out_specs, check_vma=False
    )
```

```python
import functools

import jax
import jax.numpy as jnp
from jax import lax
from jax.experimental import pallas as pl
from jax.experimental.pallas import tpu as pltpu
from jax.sharding import Mesh, PartitionSpec as P

X, YH, ZH, ZL, TG = 4, 2, 4, 2, 4
NEAR = ("x", "yh", "zl")
FEAT = ("x", "yh", "zh", "zl")
GROUP = X * YH * ZL
DOT = dict(preferred_element_type=jnp.float32)
BF, F32 = jnp.bfloat16, jnp.float32
VMEM = pl.BlockSpec(memory_space=pltpu.VMEM)
ANY = pl.BlockSpec(memory_space=pl.ANY)
LIMIT = 24 * 1024 * 1024
FLIPS = (1, 2, 3)


def cost(flops, moved):
    return pl.CostEstimate(flops=flops, bytes_accessed=moved, transcendentals=0)


def spot_of():
    index = lax.axis_index("x")
    for name, size in (("yh", YH), ("zh", ZH), ("zl", ZL)):
        index = index * size + lax.axis_index(name)
    return index


def encode_kernel(sources, weight, bias, latent, src, wts, shift, sems):
    chunks = wts.shape[0]
    depth = wts.shape[1]
    last = pltpu.make_async_copy(bias, shift, sems.at[chunks + 1])
    last.start()
    copies = [pltpu.make_async_copy(sources, src, sems.at[chunks])]
    for i in range(chunks):
        part = weight.at[pl.ds(i * depth, depth), :]
        copies.append(pltpu.make_async_copy(part, wts.at[i], sems.at[i]))
    for copy in copies:
        copy.start()
    copies[0].wait()
    total = None
    for i in range(chunks):
        copies[i + 1].wait()
        part = jnp.dot(src[:, pl.ds(i * depth, depth)], wts[i], **DOT)
        total = part if total is None else total + part
    last.wait()
    latent[...] = jnp.maximum(total + shift[...], 0.0).astype(BF)


def load_kernel(mask, latent, dec, held, own, keep, flags, sems):
    owner = lax.axis_index("tgt")
    first = pltpu.make_async_copy(mask, flags, sems.at[TG])
    first.start()
    copies = []
    for flip in range(TG):
        peer = owner ^ flip
        copies.append(pltpu.make_async_copy(dec.at[peer], held.at[peer], sems.at[flip]))
    for copy in copies:
        copy.start()
    first.wait()
    for flip in range(TG):
        value = flags[owner, owner ^ flip].astype(F32)
        keep[flip] = jnp.full(keep.shape[1:], value, F32)
    copies[0].wait()
    rows = latent[...] * keep[0, 0:1, :].astype(BF)
    own[...] = jnp.dot(rows, held[owner], **DOT)
    for copy in copies[1:]:
        copy.wait()


def decode_kernel(keep, own, l1, l2, l3, targets, dec, out):
    owner = lax.axis_index("tgt")
    base = spot_of() * targets.shape[0]
    tok, width = out.shape
    step = 256
    rows = []
    for flip, ref in zip(FLIPS, (l1, l2, l3)):
        rows.append((owner ^ flip, ref[...] * keep[flip, 0:1, :].astype(BF)))
    row_ids = lax.broadcasted_iota(jnp.int32, (tok, 1), 0)
    for start in range(0, width, step):
        cols = pl.ds(start, step)
        total = own[:, cols]
        for peer, latent in rows:
            total = total + jnp.dot(latent, dec[peer, :, cols], **DOT)
        for r in range(targets.shape[0]):
            line = targets[r : r + 1, cols].astype(F32)
            total = total - jnp.where(row_ids == base + r, line, 0.0)
        out[:, cols] = total.astype(BF)


def gather_sum_kernel(shares, out):
    total = shares[0].astype(F32)
    for i in range(1, shares.shape[0]):
        total = total + shares[i].astype(F32)
    out[...] = total.astype(out.dtype)


def spread_kernel(s0, s1, s2, s3, out):
    total = (s0[...].astype(F32) + s1[...].astype(F32)) + (
        s2[...].astype(F32) + s3[...].astype(F32)
    )
    err = total.astype(BF)
    for i in range(out.shape[0]):
        out[i] = err


def grad_kernel(flip, keep, err, dec, out):
    peer = lax.axis_index("tgt") ^ flip
    term = lax.dot_general(err[...], dec[peer], (((1,), (1,)), ((), ())), **DOT)
    out[...] = (keep[flip, 0:1, :] * term).astype(out.dtype)


def pick_kernel(err, out):
    base = spot_of() * out.shape[0]
    block = pl.multiple_of(base // 16 * 16, 16)
    value = err[pl.ds(block, 16), :].astype(F32)
    row_ids = lax.broadcasted_iota(jnp.int32, (16, 1), 0) + block
    for r in range(out.shape[0]):
        row = jnp.sum(jnp.where(row_ids == base + r, value, 0.0), axis=0, keepdims=True)
        out[r : r + 1, :] = row.astype(out.dtype)


def swap(value, name, flip):
    size = lax.axis_size(name)
    return lax.ppermute(value, name, [(i, i ^ flip) for i in range(size)])


def in_hbm(value):
    return pltpu.with_memory_space_constraint(value, pltpu.HBM)


def call(kernel, outs, specs, flops=0, moved=0, scratch=(), out_spec=VMEM):
    return pl.pallas_call(
        kernel,
        out_shape=outs,
        in_specs=specs,
        out_specs=out_spec,
        scratch_shapes=scratch,
        cost_estimate=cost(flops, moved),
        compiler_params=pltpu.CompilerParams(vmem_limit_bytes=LIMIT),
    )


def per_device(sources, targets, enc_weight, enc_bias, dec_weight, pair_mask):
    tok, width = sources.shape[1], sources.shape[2]
    feats = enc_weight.shape[2]
    rows_local = targets.shape[1]
    rows = tok // GROUP
    shape = jax.ShapeDtypeStruct

    chunks = 3
    latent = call(
        encode_kernel,
        shape((tok, feats), BF),
        [ANY, ANY, ANY],
        2 * tok * feats * width,
        2 * feats * width,
        scratch=[
            pltpu.VMEM((tok, width), BF),
            pltpu.VMEM((chunks, width // chunks, feats), BF),
            pltpu.VMEM((1, feats), F32),
            pltpu.SemaphoreType.DMA((chunks + 2,)),
        ],
    )(in_hbm(sources[0]), in_hbm(enc_weight[0]), in_hbm(enc_bias))
    got = {flip: swap(latent, "tgt", flip) for flip in FLIPS}
    flops = 2 * tok * feats * width
    dec, own, keep = call(
        load_kernel,
        [
            shape((TG, feats, width), BF),
            shape((tok, width), F32),
            shape((TG, 8, feats), F32),
        ],
        [ANY, VMEM, ANY],
        flops,
        2 * TG * feats * width,
        scratch=[pltpu.SMEM((TG, TG), jnp.int32), pltpu.SemaphoreType.DMA((TG + 1,))],
        out_spec=[VMEM] * 3,
    )(in_hbm(pair_mask), latent, in_hbm(dec_weight[0]))
    shares = call(
        decode_kernel,
        shape((tok, width), BF),
        [VMEM] * 7,
        3 * flops,
    )(keep, own, got[1], got[2], got[3], targets[0], dec)

    shares = shares.reshape(GROUP, rows, width)
    shares = lax.all_to_all(shares, NEAR, 0, 0, tiled=True)
    near = call(gather_sum_kernel, shape((rows, width), BF), [VMEM])(shares)
    parts = [near] * ZH
    for flip in (1, 3, 2):
        parts[flip] = swap(near, "zh", flip)
    copies = call(spread_kernel, shape((GROUP, rows, width), BF), [VMEM] * 4)(*parts)
    err_full = lax.all_to_all(copies, NEAR, 0, 0, tiled=True).reshape(tok, width)

    def term(flip, kind):
        kernel = functools.partial(grad_kernel, flip)
        specs = [VMEM] * 3
        return call(kernel, shape((tok, feats), kind), specs, flops)(
            keep, err_full, dec
        )

    back = {flip: swap(term(flip, BF), "tgt", flip) for flip in (3, 2, 1)}
    grad = term(0, F32)
    err_local = call(pick_kernel, shape((rows_local, width), BF), [VMEM])(err_full)
    for flip in FLIPS:
        grad = grad + back[flip].astype(F32)
    return (err_local[None], grad.astype(BF)[None])


def solution(mesh):
    grid = Mesh(
        mesh.devices.reshape(X, YH, ZH, ZL, TG), ("x", "yh", "zh", "zl", "tgt")
    )
    in_specs = (
        P("tgt", None, None),
        P("tgt", FEAT, None),
        P("tgt", None, FEAT),
        P("tgt", FEAT),
        P("tgt", None, FEAT, None),
        P(),
    )
    out_specs = (P("tgt", FEAT, None), P("tgt", None, FEAT))
    return jax.shard_map(
        per_device, mesh=grid, in_specs=in_specs, out_specs=out_specs, check_vma=False
    )
```

```python
import functools

import jax
import jax.numpy as jnp
from jax import lax
from jax.experimental import pallas as pl
from jax.experimental.pallas import tpu as pltpu
from jax.sharding import Mesh, PartitionSpec as P


X, YH, ZH, ZL, TG = 4, 2, 4, 2, 4
NEAR = ("x", "yh", "zl")
FEAT = ("x", "yh", "zh", "zl")
GROUP = X * YH * ZL
DOT = dict(preferred_element_type=jnp.float32)
BF, F32 = jnp.bfloat16, jnp.float32
VMEM = pl.BlockSpec(memory_space=pltpu.VMEM)
ANY = pl.BlockSpec(memory_space=pl.ANY)
LIMIT = 24 * 1024 * 1024


def cost(flops, moved):
    return pl.CostEstimate(flops=flops, bytes_accessed=moved, transcendentals=0)


def spot_of():
    index = lax.axis_index("x")
    for name, size in (("yh", YH), ("zh", ZH), ("zl", ZL)):
        index = index * size + lax.axis_index(name)
    return index


def encode_kernel(sources, weight, bias, latent, src, wts, shift, sems):
    chunks = wts.shape[0]
    depth = wts.shape[1]
    last = pltpu.make_async_copy(bias, shift, sems.at[chunks + 1])
    last.start()
    copies = [pltpu.make_async_copy(sources, src, sems.at[chunks])]
    for i in range(chunks):
        part = weight.at[pl.ds(i * depth, depth), :]
        copies.append(pltpu.make_async_copy(part, wts.at[i], sems.at[i]))
    for copy in copies:
        copy.start()
    copies[0].wait()
    total = None
    for i in range(chunks):
        copies[i + 1].wait()
        part = jnp.dot(src[:, pl.ds(i * depth, depth)], wts[i], **DOT)
        total = part if total is None else total + part
    last.wait()
    latent[...] = jnp.maximum(total + shift[...], 0.0).astype(BF)


def load_kernel(mask, latent, dec, held, own, keep, flags, sems):
    owner = lax.axis_index("tgt")
    first = pltpu.make_async_copy(mask, flags, sems.at[TG])
    first.start()
    copies = []
    for flip in range(TG):
        peer = owner ^ flip
        copies.append(pltpu.make_async_copy(dec.at[peer], held.at[peer], sems.at[flip]))
    for copy in copies:
        copy.start()
    first.wait()
    for flip in range(TG):
        value = flags[owner, owner ^ flip].astype(F32)
        keep[flip] = jnp.full(keep.shape[1:], value, F32)
    copies[0].wait()
    rows = latent[...] * keep[0, 0:1, :].astype(BF)
    own[...] = jnp.dot(rows, held[owner], **DOT)
    for copy in copies[1:]:
        copy.wait()


def decode_pair_kernel(keep, own, l1, l2, dec, out):
    owner = lax.axis_index("tgt")
    step = 256
    rows = []
    for flip, ref in ((1, l1), (2, l2)):
        rows.append((owner ^ flip, ref[...] * keep[flip, 0:1, :].astype(BF)))
    for start in range(0, out.shape[1], step):
        cols = pl.ds(start, step)
        total = own[:, cols]
        for peer, latent in rows:
            total = total + jnp.dot(latent, dec[peer, :, cols], **DOT)
        out[:, cols] = total


def decode_last_kernel(keep, most, l3, targets, dec, out):
    peer = lax.axis_index("tgt") ^ 3
    base = spot_of() * targets.shape[0]
    tok, width = out.shape
    step = 256
    latent = l3[...] * keep[3, 0:1, :].astype(BF)
    row_ids = lax.broadcasted_iota(jnp.int32, (tok, 1), 0)
    for start in range(0, width, step):
        cols = pl.ds(start, step)
        total = most[:, cols] + jnp.dot(latent, dec[peer, :, cols], **DOT)
        for r in range(targets.shape[0]):
            line = targets[r : r + 1, cols].astype(F32)
            total = total - jnp.where(row_ids == base + r, line, 0.0)
        out[:, cols] = total.astype(BF)


def gather_sum_kernel(shares, out):
    total = shares[0].astype(F32)
    for i in range(1, shares.shape[0]):
        total = total + shares[i].astype(F32)
    out[...] = total.astype(out.dtype)


def spread_kernel(s0, s1, s2, s3, out):
    total = (s0[...].astype(F32) + s1[...].astype(F32)) + (
        s2[...].astype(F32) + s3[...].astype(F32)
    )
    err = total.astype(BF)
    for i in range(out.shape[0]):
        out[i] = err


def grad_kernel(flip, keep, err, dec, out):
    peer = lax.axis_index("tgt") ^ flip
    term = lax.dot_general(err[...], dec[peer], (((1,), (1,)), ((), ())), **DOT)
    out[...] = (keep[flip, 0:1, :] * term).astype(out.dtype)


def join_kernel(a, b, out):
    out[...] = (a[...] + b[...]).astype(out.dtype)


def pick_kernel(err, out):
    base = spot_of() * out.shape[0]
    block = pl.multiple_of(base // 16 * 16, 16)
    value = err[pl.ds(block, 16), :].astype(F32)
    row_ids = lax.broadcasted_iota(jnp.int32, (16, 1), 0) + block
    for r in range(out.shape[0]):
        row = jnp.sum(jnp.where(row_ids == base + r, value, 0.0), axis=0, keepdims=True)
        out[r : r + 1, :] = row.astype(out.dtype)


def swap(value, name, flip):
    size = lax.axis_size(name)
    return lax.ppermute(value, name, [(i, i ^ flip) for i in range(size)])


def in_hbm(value):
    return pltpu.with_memory_space_constraint(value, pltpu.HBM)


def call(kernel, outs, specs, flops=0, moved=0, scratch=(), out_spec=VMEM):
    return pl.pallas_call(
        kernel,
        out_shape=outs,
        in_specs=specs,
        out_specs=out_spec,
        scratch_shapes=scratch,
        cost_estimate=cost(flops, moved),
        compiler_params=pltpu.CompilerParams(vmem_limit_bytes=LIMIT),
    )


def per_device(sources, targets, enc_weight, enc_bias, dec_weight, pair_mask):
    tok, width = sources.shape[1], sources.shape[2]
    feats = enc_weight.shape[2]
    rows_local = targets.shape[1]
    rows = tok // GROUP
    shape = jax.ShapeDtypeStruct

    chunks = 3
    latent = call(
        encode_kernel,
        shape((tok, feats), BF),
        [ANY, ANY, ANY],
        2 * tok * feats * width,
        2 * feats * width,
        scratch=[
            pltpu.VMEM((tok, width), BF),
            pltpu.VMEM((chunks, width // chunks, feats), BF),
            pltpu.VMEM((1, feats), F32),
            pltpu.SemaphoreType.DMA((chunks + 2,)),
        ],
    )(in_hbm(sources[0]), in_hbm(enc_weight[0]), in_hbm(enc_bias))
    l2 = swap(latent, "tgt", 2)
    l1 = swap(latent, "tgt", 1)
    flops = 2 * tok * feats * width
    load = call(
        load_kernel,
        [
            shape((TG, feats, width), BF),
            shape((tok, width), F32),
            shape((TG, 8, feats), F32),
        ],
        [ANY, VMEM, ANY],
        flops,
        2 * TG * feats * width,
        scratch=[pltpu.SMEM((TG, TG), jnp.int32), pltpu.SemaphoreType.DMA((TG + 1,))],
        out_spec=[VMEM] * 3,
    )
    dec, own, keep = load(in_hbm(pair_mask), latent, in_hbm(dec_weight[0]))
    l3 = swap(l2, "tgt", 1)
    most = call(decode_pair_kernel, shape((tok, width), F32), [VMEM] * 5, 2 * flops)(
        keep, own, l1, l2, dec
    )
    shares = call(decode_last_kernel, shape((tok, width), BF), [VMEM] * 5, flops)(
        keep, most, l3, targets[0], dec
    )

    shares = shares.reshape(GROUP, rows, width)
    shares = lax.all_to_all(shares, NEAR, 0, 0, tiled=True)
    near = call(gather_sum_kernel, shape((rows, width), BF), [VMEM])(shares)
    parts = [near] * ZH
    for flip in (2, 3, 1):
        parts[flip] = swap(near, "zh", flip)
    copies = call(spread_kernel, shape((GROUP, rows, width), BF), [VMEM] * 4)(*parts)
    err_full = lax.all_to_all(copies, NEAR, 0, 0, tiled=True).reshape(tok, width)

    def term(flip, kind):
        kernel = functools.partial(grad_kernel, flip)
        specs = [VMEM] * 3
        return call(kernel, shape((tok, feats), kind), specs, flops)(
            keep, err_full, dec
        )

    diag = term(3, F32)
    diag = swap(diag, "tgt", 1)
    far = term(2, F32)
    far = call(join_kernel, shape((tok, feats), BF), [VMEM] * 2)(far, diag)
    far = swap(far, "tgt", 2)
    near = term(1, F32)
    near = swap(near, "tgt", 1)
    own = term(0, F32)
    err_local = call(pick_kernel, shape((rows_local, width), BF), [VMEM])(err_full)
    grad = own + near + far.astype(F32)
    return (err_local[None], grad.astype(BF)[None])


def solution(mesh):
    grid = Mesh(
        mesh.devices.reshape(X, YH, ZH, ZL, TG), ("x", "yh", "zh", "zl", "tgt")
    )
    in_specs = (
        P("tgt", None, None),
        P("tgt", FEAT, None),
        P("tgt", None, FEAT),
        P("tgt", FEAT),
        P("tgt", None, FEAT, None),
        P(),
    )
    out_specs = (P("tgt", FEAT, None), P("tgt", None, FEAT))
    return jax.shard_map(
        per_device, mesh=grid, in_specs=in_specs, out_specs=out_specs, check_vma=False
    )
```

```python
import functools

import jax
import jax.numpy as jnp
from jax import lax
from jax.experimental import pallas as pl
from jax.experimental.pallas import tpu as pltpu
from jax.sharding import Mesh, PartitionSpec as P


X, YH, ZH, ZL, TG = 4, 2, 4, 2, 4
NEAR = ("x", "yh", "zl")
FEAT = ("x", "yh", "zh", "zl")
GROUP = X * YH * ZL
DOT = dict(preferred_element_type=jnp.float32)
BF, F32 = jnp.bfloat16, jnp.float32
VMEM = pl.BlockSpec(memory_space=pltpu.VMEM)
ANY = pl.BlockSpec(memory_space=pl.ANY)
LIMIT = 24 * 1024 * 1024
FLIPS = (1, 2, 3)


def cost(flops, moved):
    return pl.CostEstimate(flops=flops, bytes_accessed=moved, transcendentals=0)


def spot_of():
    index = lax.axis_index("x")
    for name, size in (("yh", YH), ("zh", ZH), ("zl", ZL)):
        index = index * size + lax.axis_index(name)
    return index


def encode_kernel(sources, weight, bias, dec, latent, mine, src, wts, shift, sems):
    chunks = wts.shape[0]
    depth = wts.shape[1]
    copies = [pltpu.make_async_copy(sources, src, sems.at[chunks])]
    for i in range(chunks):
        part = weight.at[pl.ds(i * depth, depth), :]
        copies.append(pltpu.make_async_copy(part, wts.at[i], sems.at[i]))
    late = [
        pltpu.make_async_copy(bias, shift, sems.at[chunks + 1]),
        pltpu.make_async_copy(dec.at[lax.axis_index("tgt")], mine, sems.at[chunks + 2]),
    ]
    for copy in copies + late:
        copy.start()
    copies[0].wait()
    total = None
    for i in range(chunks):
        copies[i + 1].wait()
        part = jnp.dot(src[:, pl.ds(i * depth, depth)], wts[i], **DOT)
        total = part if total is None else total + part
    late[0].wait()
    latent[...] = jnp.maximum(total + shift[...], 0.0).astype(BF)
    late[1].wait()


def load_kernel(mask, latent, mine, dec, held, own, keep, flags, sems):
    owner = lax.axis_index("tgt")
    first = pltpu.make_async_copy(mask, flags, sems.at[0])
    first.start()
    copies = []
    for flip in FLIPS:
        peer = owner ^ flip
        copies.append(
            pltpu.make_async_copy(dec.at[peer], held.at[flip - 1], sems.at[flip])
        )
    for copy in copies:
        copy.start()
    first.wait()
    for flip in range(TG):
        value = flags[owner, owner ^ flip].astype(F32)
        keep[flip] = jnp.full(keep.shape[1:], value, F32)
    rows = latent[...] * keep[0, 0:1, :].astype(BF)
    own[...] = jnp.dot(rows, mine[...], **DOT)
    for copy in copies:
        copy.wait()


def decode_pair_kernel(keep, own, l1, l2, dec, out):
    step = 256
    rows = []
    for flip, ref in ((1, l1), (2, l2)):
        rows.append((flip - 1, ref[...] * keep[flip, 0:1, :].astype(BF)))
    for start in range(0, out.shape[1], step):
        cols = pl.ds(start, step)
        total = own[:, cols]
        for slab, latent in rows:
            total = total + jnp.dot(latent, dec[slab, :, cols], **DOT)
        out[:, cols] = total


def decode_last_kernel(keep, most, l3, targets, dec, out):
    base = spot_of() * targets.shape[0]
    tok, width = out.shape
    step = 256
    latent = l3[...] * keep[3, 0:1, :].astype(BF)
    row_ids = lax.broadcasted_iota(jnp.int32, (tok, 1), 0)
    for start in range(0, width, step):
        cols = pl.ds(start, step)
        total = most[:, cols] + jnp.dot(latent, dec[2, :, cols], **DOT)
        for r in range(targets.shape[0]):
            line = targets[r : r + 1, cols].astype(F32)
            total = total - jnp.where(row_ids == base + r, line, 0.0)
        out[:, cols] = total.astype(BF)


def gather_sum_kernel(shares, out):
    total = shares[0].astype(F32)
    for i in range(1, shares.shape[0]):
        total = total + shares[i].astype(F32)
    out[...] = total.astype(out.dtype)


def pair_kernel(a, b, out):
    out[...] = a[...].astype(F32) + b[...].astype(F32)


def spread_kernel(a, b, out):
    err = (a[...] + b[...]).astype(BF)
    for i in range(out.shape[0]):
        out[i] = err


def grad_kernel(flip, keep, err, dec, out):
    slab = dec[flip - 1] if flip else dec[...]
    term = lax.dot_general(err[...], slab, (((1,), (1,)), ((), ())), **DOT)
    out[...] = (keep[flip, 0:1, :] * term).astype(out.dtype)


def join_kernel(a, b, out):
    out[...] = (a[...] + b[...]).astype(out.dtype)


def pick_kernel(err, out):
    base = spot_of() * out.shape[0]
    block = pl.multiple_of(base // 16 * 16, 16)
    value = err[pl.ds(block, 16), :].astype(F32)
    row_ids = lax.broadcasted_iota(jnp.int32, (16, 1), 0) + block
    for r in range(out.shape[0]):
        row = jnp.sum(jnp.where(row_ids == base + r, value, 0.0), axis=0, keepdims=True)
        out[r : r + 1, :] = row.astype(out.dtype)


def swap(value, name, flip):
    size = lax.axis_size(name)
    return lax.ppermute(value, name, [(i, i ^ flip) for i in range(size)])


def in_hbm(value):
    return pltpu.with_memory_space_constraint(value, pltpu.HBM)


def call(kernel, outs, specs, flops=0, moved=0, scratch=(), out_spec=VMEM):
    return pl.pallas_call(
        kernel,
        out_shape=outs,
        in_specs=specs,
        out_specs=out_spec,
        scratch_shapes=scratch,
        cost_estimate=cost(flops, moved),
        compiler_params=pltpu.CompilerParams(vmem_limit_bytes=LIMIT),
    )


def per_device(sources, targets, enc_weight, enc_bias, dec_weight, pair_mask):
    tok, width = sources.shape[1], sources.shape[2]
    feats = enc_weight.shape[2]
    rows_local = targets.shape[1]
    rows = tok // GROUP
    shape = jax.ShapeDtypeStruct

    chunks = 3
    slabs = in_hbm(dec_weight[0])
    latent, mine = call(
        encode_kernel,
        [shape((tok, feats), BF), shape((feats, width), BF)],
        [ANY] * 4,
        2 * tok * feats * width,
        2 * feats * width,
        scratch=[
            pltpu.VMEM((tok, width), BF),
            pltpu.VMEM((chunks, width // chunks, feats), BF),
            pltpu.VMEM((1, feats), F32),
            pltpu.SemaphoreType.DMA((chunks + 3,)),
        ],
        out_spec=[VMEM] * 2,
    )(in_hbm(sources[0]), in_hbm(enc_weight[0]), in_hbm(enc_bias), slabs)
    l2 = swap(latent, "tgt", 2)
    l1 = swap(latent, "tgt", 1)
    flops = 2 * tok * feats * width
    load = call(
        load_kernel,
        [
            shape((TG - 1, feats, width), BF),
            shape((tok, width), F32),
            shape((TG, 8, feats), F32),
        ],
        [ANY, VMEM, VMEM, ANY],
        flops,
        2 * TG * feats * width,
        scratch=[pltpu.SMEM((TG, TG), jnp.int32), pltpu.SemaphoreType.DMA((TG,))],
        out_spec=[VMEM] * 3,
    )
    dec, own, keep = load(in_hbm(pair_mask), latent, mine, slabs)
    l3 = swap(l2, "tgt", 1)
    most = call(decode_pair_kernel, shape((tok, width), F32), [VMEM] * 5, 2 * flops)(
        keep, own, l1, l2, dec
    )
    shares = call(decode_last_kernel, shape((tok, width), BF), [VMEM] * 5, flops)(
        keep, most, l3, targets[0], dec
    )

    shares = shares.reshape(GROUP, rows, width)
    shares = lax.all_to_all(shares, NEAR, 0, 0, tiled=True)
    near = call(gather_sum_kernel, shape((rows, width), BF), [VMEM])(shares)
    other = swap(near, "zh", 1)
    pair = call(pair_kernel, shape((rows, width), F32), [VMEM] * 2)(near, other)
    other = swap(pair, "zh", 3)
    copies = call(spread_kernel, shape((GROUP, rows, width), BF), [VMEM] * 2)(pair, other)
    err_full = lax.all_to_all(copies, NEAR, 0, 0, tiled=True).reshape(tok, width)

    def term(flip, kind):
        kernel = functools.partial(grad_kernel, flip)
        specs = [VMEM] * 3
        return call(kernel, shape((tok, feats), kind), specs, flops)(
            keep, err_full, dec if flip else mine
        )

    diag = term(3, F32)
    diag = swap(diag, "tgt", 1)
    far = term(2, F32)
    far = call(join_kernel, shape((tok, feats), BF), [VMEM] * 2)(far, diag)
    far = swap(far, "tgt", 2)
    near = term(1, F32)
    near = swap(near, "tgt", 1)
    own = term(0, F32)
    err_local = call(pick_kernel, shape((rows_local, width), BF), [VMEM])(err_full)
    grad = own + near + far.astype(F32)
    return (err_local[None], grad.astype(BF)[None])


def solution(mesh):
    grid = Mesh(
        mesh.devices.reshape(X, YH, ZH, ZL, TG), ("x", "yh", "zh", "zl", "tgt")
    )
    in_specs = (
        P("tgt", None, None),
        P("tgt", FEAT, None),
        P("tgt", None, FEAT),
        P("tgt", FEAT),
        P("tgt", None, FEAT, None),
        P(),
    )
    out_specs = (P("tgt", FEAT, None), P("tgt", None, FEAT))
    return jax.shard_map(
        per_device, mesh=grid, in_specs=in_specs, out_specs=out_specs, check_vma=False
    )
```

```python
import functools

import jax
import jax.numpy as jnp
from jax import lax
from jax.experimental import pallas as pl
from jax.experimental.pallas import tpu as pltpu
from jax.sharding import Mesh, PartitionSpec as P


X, YH, ZH, ZL, TG = 4, 2, 4, 2, 4
NEAR = ("x", "yh", "zl")
FEAT = ("x", "yh", "zh", "zl")
GROUP = X * YH * ZL
DOT = dict(preferred_element_type=jnp.float32)
BF, F32 = jnp.bfloat16, jnp.float32
VMEM = pl.BlockSpec(memory_space=pltpu.VMEM)
ANY = pl.BlockSpec(memory_space=pl.ANY)
LIMIT = 24 * 1024 * 1024
FLIPS = (1, 2, 3)


def cost(flops, moved):
    return pl.CostEstimate(flops=flops, bytes_accessed=moved, transcendentals=0)


def spot_of():
    index = lax.axis_index("x")
    for name, size in (("yh", YH), ("zh", ZH), ("zl", ZL)):
        index = index * size + lax.axis_index(name)
    return index


def encode_kernel(sources, weight, bias, dec, latent, mine, src, wts, shift, sems):
    chunks = wts.shape[0]
    depth = wts.shape[1]
    copies = [pltpu.make_async_copy(sources, src, sems.at[chunks])]
    for i in range(chunks):
        part = weight.at[pl.ds(i * depth, depth), :]
        copies.append(pltpu.make_async_copy(part, wts.at[i], sems.at[i]))
    late = [
        pltpu.make_async_copy(bias, shift, sems.at[chunks + 1]),
        pltpu.make_async_copy(dec.at[lax.axis_index("tgt")], mine, sems.at[chunks + 2]),
    ]
    for copy in copies + late:
        copy.start()
    copies[0].wait()
    total = None
    for i in range(chunks):
        copies[i + 1].wait()
        part = jnp.dot(src[:, pl.ds(i * depth, depth)], wts[i], **DOT)
        total = part if total is None else total + part
    late[0].wait()
    latent[...] = jnp.maximum(total + shift[...], 0.0).astype(BF)
    late[1].wait()


def load_kernel(mask, latent, mine, dec, held, own, keep, flags, sems):
    owner = lax.axis_index("tgt")
    first = pltpu.make_async_copy(mask, flags, sems.at[0])
    first.start()
    copies = []
    for flip in FLIPS:
        peer = owner ^ flip
        copies.append(
            pltpu.make_async_copy(dec.at[peer], held.at[flip - 1], sems.at[flip])
        )
    for copy in copies:
        copy.start()
    first.wait()
    for flip in range(TG):
        value = flags[owner, owner ^ flip].astype(F32)
        keep[flip] = jnp.full(keep.shape[1:], value, F32)
    rows = latent[...] * keep[0, 0:1, :].astype(BF)
    own[...] = jnp.dot(rows, mine[...], **DOT)
    for copy in copies:
        copy.wait()


def decode_pair_kernel(keep, own, l1, l2, dec, out):
    step = 256
    rows = []
    for flip, ref in ((1, l1), (2, l2)):
        rows.append((flip - 1, ref[...] * keep[flip, 0:1, :].astype(BF)))
    for start in range(0, out.shape[1], step):
        cols = pl.ds(start, step)
        total = own[:, cols]
        for slab, latent in rows:
            total = total + jnp.dot(latent, dec[slab, :, cols], **DOT)
        out[:, cols] = total


def decode_last_kernel(keep, most, l3, targets, dec, out):
    base = spot_of() * targets.shape[0]
    tok, width = out.shape
    step = 256
    latent = l3[...] * keep[3, 0:1, :].astype(BF)
    row_ids = lax.broadcasted_iota(jnp.int32, (tok, 1), 0)
    for start in range(0, width, step):
        cols = pl.ds(start, step)
        total = most[:, cols] + jnp.dot(latent, dec[2, :, cols], **DOT)
        for r in range(targets.shape[0]):
            line = targets[r : r + 1, cols].astype(F32)
            total = total - jnp.where(row_ids == base + r, line, 0.0)
        out[:, cols] = total.astype(BF)


def gather_sum_kernel(shares, out):
    total = shares[0].astype(F32)
    for i in range(1, shares.shape[0]):
        total = total + shares[i].astype(F32)
    out[...] = total.astype(out.dtype)


def spread_kernel(s0, s1, s2, s3, out):
    total = (s0[...].astype(F32) + s1[...].astype(F32)) + (
        s2[...].astype(F32) + s3[...].astype(F32)
    )
    err = total.astype(BF)
    for i in range(out.shape[0]):
        out[i] = err


def grad_kernel(flip, keep, err, dec, out):
    slab = dec[flip - 1] if flip else dec[...]
    term = lax.dot_general(err[...], slab, (((1,), (1,)), ((), ())), **DOT)
    out[...] = (keep[flip, 0:1, :] * term).astype(out.dtype)


def join_kernel(a, b, out):
    out[...] = (a[...] + b[...]).astype(out.dtype)


def pick_kernel(err, out):
    base = spot_of() * out.shape[0]
    block = pl.multiple_of(base // 16 * 16, 16)
    value = err[pl.ds(block, 16), :].astype(F32)
    row_ids = lax.broadcasted_iota(jnp.int32, (16, 1), 0) + block
    for r in range(out.shape[0]):
        row = jnp.sum(jnp.where(row_ids == base + r, value, 0.0), axis=0, keepdims=True)
        out[r : r + 1, :] = row.astype(out.dtype)


def swap(value, name, flip):
    size = lax.axis_size(name)
    return lax.ppermute(value, name, [(i, i ^ flip) for i in range(size)])


def in_hbm(value):
    return pltpu.with_memory_space_constraint(value, pltpu.HBM)


def call(kernel, outs, specs, flops=0, moved=0, scratch=(), out_spec=VMEM):
    return pl.pallas_call(
        kernel,
        out_shape=outs,
        in_specs=specs,
        out_specs=out_spec,
        scratch_shapes=scratch,
        cost_estimate=cost(flops, moved),
        compiler_params=pltpu.CompilerParams(vmem_limit_bytes=LIMIT),
    )


def per_device(sources, targets, enc_weight, enc_bias, dec_weight, pair_mask):
    tok, width = sources.shape[1], sources.shape[2]
    feats = enc_weight.shape[2]
    rows_local = targets.shape[1]
    rows = tok // GROUP
    shape = jax.ShapeDtypeStruct

    chunks = 3
    slabs = in_hbm(dec_weight[0])
    latent, mine = call(
        encode_kernel,
        [shape((tok, feats), BF), shape((feats, width), BF)],
        [ANY] * 4,
        2 * tok * feats * width,
        2 * feats * width,
        scratch=[
            pltpu.VMEM((tok, width), BF),
            pltpu.VMEM((chunks, width // chunks, feats), BF),
            pltpu.VMEM((1, feats), F32),
            pltpu.SemaphoreType.DMA((chunks + 3,)),
        ],
        out_spec=[VMEM] * 2,
    )(in_hbm(sources[0]), in_hbm(enc_weight[0]), in_hbm(enc_bias), slabs)
    l2 = swap(latent, "tgt", 2)
    l1 = swap(latent, "tgt", 1)
    flops = 2 * tok * feats * width
    load = call(
        load_kernel,
        [
            shape((TG - 1, feats, width), BF),
            shape((tok, width), F32),
            shape((TG, 8, feats), F32),
        ],
        [ANY, VMEM, VMEM, ANY],
        flops,
        2 * TG * feats * width,
        scratch=[pltpu.SMEM((TG, TG), jnp.int32), pltpu.SemaphoreType.DMA((TG,))],
        out_spec=[VMEM] * 3,
    )
    dec, own, keep = load(in_hbm(pair_mask), latent, mine, slabs)
    l3 = swap(l2, "tgt", 1)
    most = call(decode_pair_kernel, shape((tok, width), F32), [VMEM] * 5, 2 * flops)(
        keep, own, l1, l2, dec
    )
    shares = call(decode_last_kernel, shape((tok, width), BF), [VMEM] * 5, flops)(
        keep, most, l3, targets[0], dec
    )

    shares = shares.reshape(GROUP, rows, width)
    shares = lax.all_to_all(shares, NEAR, 0, 0, tiled=True)
    near = call(gather_sum_kernel, shape((rows, width), BF), [VMEM])(shares)
    parts = [near] * ZH
    for flip in (2, 3, 1):
        parts[flip] = swap(near, "zh", flip)
    copies = call(spread_kernel, shape((GROUP, rows, width), BF), [VMEM] * 4)(*parts)
    err_full = lax.all_to_all(copies, NEAR, 0, 0, tiled=True).reshape(tok, width)

    def term(flip, kind):
        kernel = functools.partial(grad_kernel, flip)
        specs = [VMEM] * 3
        return call(kernel, shape((tok, feats), kind), specs, flops)(
            keep, err_full, dec if flip else mine
        )

    diag = term(3, F32)
    diag = swap(diag, "tgt", 1)
    far = term(2, F32)
    far = call(join_kernel, shape((tok, feats), BF), [VMEM] * 2)(far, diag)
    far = swap(far, "tgt", 2)
    near = term(1, F32)
    near = swap(near, "tgt", 1)
    own = term(0, F32)
    err_local = call(pick_kernel, shape((rows_local, width), BF), [VMEM])(err_full)
    grad = own + near + far.astype(F32)
    return (err_local[None], grad.astype(BF)[None])


def solution(mesh):
    grid = Mesh(
        mesh.devices.reshape(X, YH, ZH, ZL, TG), ("x", "yh", "zh", "zl", "tgt")
    )
    in_specs = (
        P("tgt", None, None),
        P("tgt", FEAT, None),
        P("tgt", None, FEAT),
        P("tgt", FEAT),
        P("tgt", None, FEAT, None),
        P(),
    )
    out_specs = (P("tgt", FEAT, None), P("tgt", None, FEAT))
    return jax.shard_map(
        per_device, mesh=grid, in_specs=in_specs, out_specs=out_specs, check_vma=False
    )
```

```python
import functools

import jax
import jax.numpy as jnp
from jax import lax
from jax.experimental import pallas as pl
from jax.experimental.pallas import tpu as pltpu
from jax.sharding import Mesh, PartitionSpec as P


X, YH, ZH, ZL, TG = 4, 2, 4, 2, 4
NEAR = ("x", "yh", "zl")
FEAT = ("x", "yh", "zh", "zl")
GROUP = X * YH * ZL
DOT = dict(preferred_element_type=jnp.float32)
BF, F32 = jnp.bfloat16, jnp.float32
VMEM = pl.BlockSpec(memory_space=pltpu.VMEM)
ANY = pl.BlockSpec(memory_space=pl.ANY)
LIMIT = 24 * 1024 * 1024
FLIPS = (1, 2, 3)


def cost(flops, moved):
    return pl.CostEstimate(flops=flops, bytes_accessed=moved, transcendentals=0)


def spot_of():
    index = lax.axis_index("x")
    for name, size in (("yh", YH), ("zh", ZH), ("zl", ZL)):
        index = index * size + lax.axis_index(name)
    return index


def encode_kernel(sources, weight, bias, dec, latent, mine, src, wts, shift, sems):
    chunks = wts.shape[0]
    depth = wts.shape[1]
    copies = [pltpu.make_async_copy(sources, src, sems.at[chunks])]
    for i in range(chunks):
        part = weight.at[pl.ds(i * depth, depth), :]
        copies.append(pltpu.make_async_copy(part, wts.at[i], sems.at[i]))
    late = [
        pltpu.make_async_copy(bias, shift, sems.at[chunks + 1]),
        pltpu.make_async_copy(dec.at[lax.axis_index("tgt")], mine, sems.at[chunks + 2]),
    ]
    for copy in copies + late:
        copy.start()
    copies[0].wait()
    total = None
    for i in range(chunks):
        copies[i + 1].wait()
        part = jnp.dot(src[:, pl.ds(i * depth, depth)], wts[i], **DOT)
        total = part if total is None else total + part
    late[0].wait()
    latent[...] = jnp.maximum(total + shift[...], 0.0).astype(BF)
    late[1].wait()


def load_kernel(mask, latent, mine, dec, held, own, keep, flags, sems):
    owner = lax.axis_index("tgt")
    first = pltpu.make_async_copy(mask, flags, sems.at[0])
    first.start()
    copies = []
    for flip in FLIPS:
        peer = owner ^ flip
        copies.append(
            pltpu.make_async_copy(dec.at[peer], held.at[flip - 1], sems.at[flip])
        )
    for copy in copies:
        copy.start()
    first.wait()
    for flip in range(TG):
        value = flags[owner, owner ^ flip].astype(F32)
        keep[flip] = jnp.full(keep.shape[1:], value, F32)
    rows = latent[...] * keep[0, 0:1, :].astype(BF)
    own[...] = jnp.dot(rows, mine[...], **DOT)
    for copy in copies:
        copy.wait()


def decode_pair_kernel(keep, own, l1, l2, dec, out):
    step = 256
    rows = []
    for flip, ref in ((1, l1), (2, l2)):
        rows.append((flip - 1, ref[...] * keep[flip, 0:1, :].astype(BF)))
    for start in range(0, out.shape[1], step):
        cols = pl.ds(start, step)
        total = own[:, cols]
        for slab, latent in rows:
            total = total + jnp.dot(latent, dec[slab, :, cols], **DOT)
        out[:, cols] = total


def decode_last_kernel(keep, most, l3, targets, dec, out):
    base = spot_of() * targets.shape[0]
    tok, width = out.shape
    step = 256
    latent = l3[...] * keep[3, 0:1, :].astype(BF)
    row_ids = lax.broadcasted_iota(jnp.int32, (tok, 1), 0)
    for start in range(0, width, step):
        cols = pl.ds(start, step)
        total = most[:, cols] + jnp.dot(latent, dec[2, :, cols], **DOT)
        for r in range(targets.shape[0]):
            line = targets[r : r + 1, cols].astype(F32)
            total = total - jnp.where(row_ids == base + r, line, 0.0)
        out[:, cols] = total.astype(BF)


def gather_sum_kernel(shares, out):
    total = shares[0].astype(F32)
    for i in range(1, shares.shape[0]):
        total = total + shares[i].astype(F32)
    out[...] = total.astype(out.dtype)


def spread_kernel(s0, s1, s2, s3, out):
    total = (s0[...].astype(F32) + s1[...].astype(F32)) + (
        s2[...].astype(F32) + s3[...].astype(F32)
    )
    err = total.astype(BF)
    for i in range(out.shape[0]):
        out[i] = err


def grad_kernel(flip, keep, err, dec, out):
    slab = dec[flip - 1] if flip else dec[...]
    term = lax.dot_general(err[...], slab, (((1,), (1,)), ((), ())), **DOT)
    out[...] = (keep[flip, 0:1, :] * term).astype(out.dtype)


def turn_kernel(dec, out):
    for flip in (2, 3):
        out[flip - 2] = dec[flip - 1].T


def turned_kernel(flip, keep, err, turned, out):
    term = jnp.dot(err[...], turned[flip - 2], **DOT)
    out[...] = (keep[flip, 0:1, :] * term).astype(out.dtype)


def pick_kernel(err, out):
    base = spot_of() * out.shape[0]
    block = pl.multiple_of(base // 16 * 16, 16)
    value = err[pl.ds(block, 16), :].astype(F32)
    row_ids = lax.broadcasted_iota(jnp.int32, (16, 1), 0) + block
    for r in range(out.shape[0]):
        row = jnp.sum(jnp.where(row_ids == base + r, value, 0.0), axis=0, keepdims=True)
        out[r : r + 1, :] = row.astype(out.dtype)


def swap(value, name, flip):
    size = lax.axis_size(name)
    return lax.ppermute(value, name, [(i, i ^ flip) for i in range(size)])


def in_hbm(value):
    return pltpu.with_memory_space_constraint(value, pltpu.HBM)


def call(kernel, outs, specs, flops=0, moved=0, scratch=(), out_spec=VMEM):
    return pl.pallas_call(
        kernel,
        out_shape=outs,
        in_specs=specs,
        out_specs=out_spec,
        scratch_shapes=scratch,
        cost_estimate=cost(flops, moved),
        compiler_params=pltpu.CompilerParams(vmem_limit_bytes=LIMIT),
    )


def per_device(sources, targets, enc_weight, enc_bias, dec_weight, pair_mask):
    tok, width = sources.shape[1], sources.shape[2]
    feats = enc_weight.shape[2]
    rows_local = targets.shape[1]
    rows = tok // GROUP
    shape = jax.ShapeDtypeStruct

    chunks = 3
    slabs = in_hbm(dec_weight[0])
    latent, mine = call(
        encode_kernel,
        [shape((tok, feats), BF), shape((feats, width), BF)],
        [ANY] * 4,
        2 * tok * feats * width,
        2 * feats * width,
        scratch=[
            pltpu.VMEM((tok, width), BF),
            pltpu.VMEM((chunks, width // chunks, feats), BF),
            pltpu.VMEM((1, feats), F32),
            pltpu.SemaphoreType.DMA((chunks + 3,)),
        ],
        out_spec=[VMEM] * 2,
    )(in_hbm(sources[0]), in_hbm(enc_weight[0]), in_hbm(enc_bias), slabs)
    l2 = swap(latent, "tgt", 2)
    l1 = swap(latent, "tgt", 1)
    flops = 2 * tok * feats * width
    load = call(
        load_kernel,
        [
            shape((TG - 1, feats, width), BF),
            shape((tok, width), F32),
            shape((TG, 8, feats), F32),
        ],
        [ANY, VMEM, VMEM, ANY],
        flops,
        2 * TG * feats * width,
        scratch=[pltpu.SMEM((TG, TG), jnp.int32), pltpu.SemaphoreType.DMA((TG,))],
        out_spec=[VMEM] * 3,
    )
    dec, own, keep = load(in_hbm(pair_mask), latent, mine, slabs)
    l3 = swap(l2, "tgt", 1)
    most = call(decode_pair_kernel, shape((tok, width), F32), [VMEM] * 5, 2 * flops)(
        keep, own, l1, l2, dec
    )
    shares = call(decode_last_kernel, shape((tok, width), BF), [VMEM] * 5, flops)(
        keep, most, l3, targets[0], dec
    )

    shares = shares.reshape(GROUP, rows, width)
    shares = lax.all_to_all(shares, NEAR, 0, 0, tiled=True)
    near = call(gather_sum_kernel, shape((rows, width), BF), [VMEM])(shares)
    parts = [near] * ZH
    for flip in (2, 3, 1):
        parts[flip] = swap(near, "zh", flip)
    turned = call(turn_kernel, shape((2, width, feats), BF), [VMEM])(dec)
    copies = call(spread_kernel, shape((GROUP, rows, width), BF), [VMEM] * 4)(*parts)
    err_full = lax.all_to_all(copies, NEAR, 0, 0, tiled=True).reshape(tok, width)

    def term(flip, kind):
        far = flip > 1
        kernel = functools.partial(turned_kernel if far else grad_kernel, flip)
        slab = turned if far else dec if flip else mine
        return call(kernel, shape((tok, feats), kind), [VMEM] * 3, flops)(
            keep, err_full, slab
        )

    back = {}
    for flip in (3, 2, 1):
        part = term(flip, BF)
        back[flip] = swap(part, "tgt", flip)
    grad = term(0, F32)
    err_local = call(pick_kernel, shape((rows_local, width), BF), [VMEM])(err_full)
    for flip in FLIPS:
        grad = grad + back[flip].astype(F32)
    return (err_local[None], grad.astype(BF)[None])


def solution(mesh):
    grid = Mesh(
        mesh.devices.reshape(X, YH, ZH, ZL, TG), ("x", "yh", "zh", "zl", "tgt")
    )
    in_specs = (
        P("tgt", None, None),
        P("tgt", FEAT, None),
        P("tgt", None, FEAT),
        P("tgt", FEAT),
        P("tgt", None, FEAT, None),
        P(),
    )
    out_specs = (P("tgt", FEAT, None), P("tgt", None, FEAT))
    return jax.shard_map(
        per_device, mesh=grid, in_specs=in_specs, out_specs=out_specs, check_vma=False
    )
```

```python
import functools

import jax
import jax.numpy as jnp
from jax import lax
from jax.experimental import pallas as pl
from jax.experimental.pallas import tpu as pltpu
from jax.sharding import Mesh, PartitionSpec as P


X, YH, ZH, ZL, TG = 4, 2, 4, 2, 4
NEAR = ("x", "zl")
FEAT = ("x", "yh", "zh", "zl")
GROUP = X * ZL
DOT = dict(preferred_element_type=jnp.float32)
BF, F32 = jnp.bfloat16, jnp.float32
VMEM = pl.BlockSpec(memory_space=pltpu.VMEM)
ANY = pl.BlockSpec(memory_space=pl.ANY)
LIMIT = 24 * 1024 * 1024
FLIPS = (1, 2, 3)


def cost(flops, moved):
    return pl.CostEstimate(flops=flops, bytes_accessed=moved, transcendentals=0)


def spot_of():
    index = lax.axis_index("x")
    for name, size in (("yh", YH), ("zh", ZH), ("zl", ZL)):
        index = index * size + lax.axis_index(name)
    return index


def encode_kernel(sources, weight, bias, dec, latent, mine, src, wts, shift, sems):
    chunks = wts.shape[0]
    depth = wts.shape[1]
    copies = [pltpu.make_async_copy(sources, src, sems.at[chunks])]
    for i in range(chunks):
        part = weight.at[pl.ds(i * depth, depth), :]
        copies.append(pltpu.make_async_copy(part, wts.at[i], sems.at[i]))
    late = [
        pltpu.make_async_copy(bias, shift, sems.at[chunks + 1]),
        pltpu.make_async_copy(dec.at[lax.axis_index("tgt")], mine, sems.at[chunks + 2]),
    ]
    for copy in copies + late:
        copy.start()
    copies[0].wait()
    total = None
    for i in range(chunks):
        copies[i + 1].wait()
        part = jnp.dot(src[:, pl.ds(i * depth, depth)], wts[i], **DOT)
        total = part if total is None else total + part
    late[0].wait()
    latent[...] = jnp.maximum(total + shift[...], 0.0).astype(BF)
    late[1].wait()


def load_kernel(mask, latent, mine, dec, held, own, keep, flags, sems):
    owner = lax.axis_index("tgt")
    first = pltpu.make_async_copy(mask, flags, sems.at[0])
    first.start()
    copies = []
    for flip in FLIPS:
        peer = owner ^ flip
        copies.append(
            pltpu.make_async_copy(dec.at[peer], held.at[flip - 1], sems.at[flip])
        )
    for copy in copies:
        copy.start()
    first.wait()
    for flip in range(TG):
        value = flags[owner, owner ^ flip].astype(F32)
        keep[flip] = jnp.full(keep.shape[1:], value, F32)
    rows = latent[...] * keep[0, 0:1, :].astype(BF)
    own[...] = jnp.dot(rows, mine[...], **DOT)
    for copy in copies:
        copy.wait()


def decode_pair_kernel(keep, own, l1, l2, dec, out):
    step = 256
    rows = []
    for flip, ref in ((1, l1), (2, l2)):
        rows.append((flip - 1, ref[...] * keep[flip, 0:1, :].astype(BF)))
    for start in range(0, out.shape[1], step):
        cols = pl.ds(start, step)
        total = own[:, cols]
        for slab, latent in rows:
            total = total + jnp.dot(latent, dec[slab, :, cols], **DOT)
        out[:, cols] = total


def decode_last_kernel(keep, most, l3, targets, dec, out):
    base = spot_of() * targets.shape[0]
    tok, width = out.shape
    step = 256
    latent = l3[...] * keep[3, 0:1, :].astype(BF)
    row_ids = lax.broadcasted_iota(jnp.int32, (tok, 1), 0)
    for start in range(0, width, step):
        cols = pl.ds(start, step)
        total = most[:, cols] + jnp.dot(latent, dec[2, :, cols], **DOT)
        for r in range(targets.shape[0]):
            line = targets[r : r + 1, cols].astype(F32)
            total = total - jnp.where(row_ids == base + r, line, 0.0)
        out[:, cols] = total.astype(BF)


def gather_sum_kernel(shares, out):
    total = shares[0].astype(F32)
    for i in range(1, shares.shape[0]):
        total = total + shares[i].astype(F32)
    out[...] = total.astype(out.dtype)


def pair_kernel(a, b, out):
    out[...] = (a[...].astype(F32) + b[...].astype(F32)).astype(out.dtype)


def spread_kernel(s0, s1, s2, s3, out):
    total = (s0[...].astype(F32) + s1[...].astype(F32)) + (
        s2[...].astype(F32) + s3[...].astype(F32)
    )
    err = total.astype(BF)
    for i in range(out.shape[0]):
        out[i] = err


def grad_kernel(flip, keep, err, dec, out):
    slab = dec[flip - 1] if flip else dec[...]
    term = lax.dot_general(err[...], slab, (((1,), (1,)), ((), ())), **DOT)
    out[...] = (keep[flip, 0:1, :] * term).astype(out.dtype)


def turn_kernel(dec, out):
    for flip in (2, 3):
        out[flip - 2] = dec[flip - 1].T


def turned_kernel(flip, keep, err, turned, out):
    term = jnp.dot(err[...], turned[flip - 2], **DOT)
    out[...] = (keep[flip, 0:1, :] * term).astype(out.dtype)


def pick_kernel(err, out):
    base = spot_of() * out.shape[0]
    block = pl.multiple_of(base // 16 * 16, 16)
    value = err[pl.ds(block, 16), :].astype(F32)
    row_ids = lax.broadcasted_iota(jnp.int32, (16, 1), 0) + block
    for r in range(out.shape[0]):
        row = jnp.sum(jnp.where(row_ids == base + r, value, 0.0), axis=0, keepdims=True)
        out[r : r + 1, :] = row.astype(out.dtype)


def swap(value, name, flip):
    size = lax.axis_size(name)
    return lax.ppermute(value, name, [(i, i ^ flip) for i in range(size)])


def in_hbm(value):
    return pltpu.with_memory_space_constraint(value, pltpu.HBM)


def call(kernel, outs, specs, flops=0, moved=0, scratch=(), out_spec=VMEM):
    return pl.pallas_call(
        kernel,
        out_shape=outs,
        in_specs=specs,
        out_specs=out_spec,
        scratch_shapes=scratch,
        cost_estimate=cost(flops, moved),
        compiler_params=pltpu.CompilerParams(vmem_limit_bytes=LIMIT),
    )


def per_device(sources, targets, enc_weight, enc_bias, dec_weight, pair_mask):
    tok, width = sources.shape[1], sources.shape[2]
    feats = enc_weight.shape[2]
    rows_local = targets.shape[1]
    rows = tok // GROUP
    shape = jax.ShapeDtypeStruct

    chunks = 3
    slabs = in_hbm(dec_weight[0])
    latent, mine = call(
        encode_kernel,
        [shape((tok, feats), BF), shape((feats, width), BF)],
        [ANY] * 4,
        2 * tok * feats * width,
        2 * feats * width,
        scratch=[
            pltpu.VMEM((tok, width), BF),
            pltpu.VMEM((chunks, width // chunks, feats), BF),
            pltpu.VMEM((1, feats), F32),
            pltpu.SemaphoreType.DMA((chunks + 3,)),
        ],
        out_spec=[VMEM] * 2,
    )(in_hbm(sources[0]), in_hbm(enc_weight[0]), in_hbm(enc_bias), slabs)
    l2 = swap(latent, "tgt", 2)
    l1 = swap(latent, "tgt", 1)
    flops = 2 * tok * feats * width
    load = call(
        load_kernel,
        [
            shape((TG - 1, feats, width), BF),
            shape((tok, width), F32),
            shape((TG, 8, feats), F32),
        ],
        [ANY, VMEM, VMEM, ANY],
        flops,
        2 * TG * feats * width,
        scratch=[pltpu.SMEM((TG, TG), jnp.int32), pltpu.SemaphoreType.DMA((TG,))],
        out_spec=[VMEM] * 3,
    )
    dec, own, keep = load(in_hbm(pair_mask), latent, mine, slabs)
    l3 = swap(l2, "tgt", 1)
    most = call(decode_pair_kernel, shape((tok, width), F32), [VMEM] * 5, 2 * flops)(
        keep, own, l1, l2, dec
    )
    shares = call(decode_last_kernel, shape((tok, width), BF), [VMEM] * 5, flops)(
        keep, most, l3, targets[0], dec
    )

    shares = shares.reshape(GROUP, rows, width)
    shares = lax.all_to_all(shares, NEAR, 0, 0, tiled=True)
    near = call(gather_sum_kernel, shape((rows, width), BF), [VMEM])(shares)
    other = swap(near, "yh", 1)
    near = call(pair_kernel, shape((rows, width), BF), [VMEM] * 2)(near, other)
    parts = [near] * ZH
    for flip in (2, 3, 1):
        parts[flip] = swap(near, "zh", flip)
    turned = call(turn_kernel, shape((2, width, feats), BF), [VMEM])(dec)
    copies = call(spread_kernel, shape((GROUP, rows, width), BF), [VMEM] * 4)(*parts)
    err_full = lax.all_to_all(copies, NEAR, 0, 0, tiled=True).reshape(tok, width)

    def term(flip, kind):
        far = flip > 1
        kernel = functools.partial(turned_kernel if far else grad_kernel, flip)
        slab = turned if far else dec if flip else mine
        return call(kernel, shape((tok, feats), kind), [VMEM] * 3, flops)(
            keep, err_full, slab
        )

    back = {}
    for flip in (3, 2, 1):
        part = term(flip, BF)
        back[flip] = swap(part, "tgt", flip)
    grad = term(0, F32)
    err_local = call(pick_kernel, shape((rows_local, width), BF), [VMEM])(err_full)
    for flip in FLIPS:
        grad = grad + back[flip].astype(F32)
    return (err_local[None], grad.astype(BF)[None])


def solution(mesh):
    grid = Mesh(
        mesh.devices.reshape(X, YH, ZH, ZL, TG), ("x", "yh", "zh", "zl", "tgt")
    )
    in_specs = (
        P("tgt", None, None),
        P("tgt", FEAT, None),
        P("tgt", None, FEAT),
        P("tgt", FEAT),
        P("tgt", None, FEAT, None),
        P(),
    )
    out_specs = (P("tgt", FEAT, None), P("tgt", None, FEAT))
    return jax.shard_map(
        per_device, mesh=grid, in_specs=in_specs, out_specs=out_specs, check_vma=False
    )
```

```python
import functools

import jax
import jax.numpy as jnp
from jax import lax
from jax.experimental import pallas as pl
from jax.experimental.pallas import tpu as pltpu
from jax.sharding import Mesh, PartitionSpec as P


X, YH, ZH, ZL, TG = 4, 2, 4, 2, 4
NEAR = ("x", "yh", "zl")
FEAT = ("x", "yh", "zh", "zl")
GROUP = X * YH * ZL
DOT = dict(preferred_element_type=jnp.float32)
BF, F32 = jnp.bfloat16, jnp.float32
VMEM = pl.BlockSpec(memory_space=pltpu.VMEM)
ANY = pl.BlockSpec(memory_space=pl.ANY)
LIMIT = 24 * 1024 * 1024
FLIPS = (1, 2, 3)


def cost(flops, moved):
    return pl.CostEstimate(flops=flops, bytes_accessed=moved, transcendentals=0)


def spot_of():
    index = lax.axis_index("x")
    for name, size in (("yh", YH), ("zh", ZH), ("zl", ZL)):
        index = index * size + lax.axis_index(name)
    return index


def encode_kernel(sources, weight, bias, dec, latent, mine, src, wts, shift, sems):
    chunks = wts.shape[0]
    depth = wts.shape[1]
    copies = [pltpu.make_async_copy(sources, src, sems.at[chunks])]
    for i in range(chunks):
        part = weight.at[pl.ds(i * depth, depth), :]
        copies.append(pltpu.make_async_copy(part, wts.at[i], sems.at[i]))
    late = [
        pltpu.make_async_copy(bias, shift, sems.at[chunks + 1]),
        pltpu.make_async_copy(dec.at[lax.axis_index("tgt")], mine, sems.at[chunks + 2]),
    ]
    for copy in copies + late:
        copy.start()
    copies[0].wait()
    total = None
    for i in range(chunks):
        copies[i + 1].wait()
        part = jnp.dot(src[:, pl.ds(i * depth, depth)], wts[i], **DOT)
        total = part if total is None else total + part
    late[0].wait()
    latent[...] = jnp.maximum(total + shift[...], 0.0).astype(BF)
    late[1].wait()


def load_kernel(mask, latent, mine, dec, held, own, keep, flags, sems):
    owner = lax.axis_index("tgt")
    first = pltpu.make_async_copy(mask, flags, sems.at[0])
    first.start()
    copies = []
    for flip in FLIPS:
        peer = owner ^ flip
        copies.append(
            pltpu.make_async_copy(dec.at[peer], held.at[flip - 1], sems.at[flip])
        )
    for copy in copies:
        copy.start()
    first.wait()
    for flip in range(TG):
        value = flags[owner, owner ^ flip].astype(F32)
        keep[flip] = jnp.full(keep.shape[1:], value, F32)
    rows = latent[...] * keep[0, 0:1, :].astype(BF)
    own[...] = jnp.dot(rows, mine[...], **DOT)
    for copy in copies:
        copy.wait()


def decode_pair_kernel(keep, own, l1, l2, dec, out):
    step = 256
    rows = []
    for flip, ref in ((1, l1), (2, l2)):
        rows.append((flip - 1, ref[...] * keep[flip, 0:1, :].astype(BF)))
    for start in range(0, out.shape[1], step):
        cols = pl.ds(start, step)
        total = own[:, cols]
        for slab, latent in rows:
            total = total + jnp.dot(latent, dec[slab, :, cols], **DOT)
        out[:, cols] = total


def decode_last_kernel(keep, most, l3, targets, dec, out):
    base = spot_of() * targets.shape[0]
    tok, width = out.shape
    step = 256
    latent = l3[...] * keep[3, 0:1, :].astype(BF)
    row_ids = lax.broadcasted_iota(jnp.int32, (tok, 1), 0)
    for start in range(0, width, step):
        cols = pl.ds(start, step)
        total = most[:, cols] + jnp.dot(latent, dec[2, :, cols], **DOT)
        for r in range(targets.shape[0]):
            line = targets[r : r + 1, cols].astype(F32)
            total = total - jnp.where(row_ids == base + r, line, 0.0)
        out[:, cols] = total.astype(BF)


def gather_sum_kernel(shares, out):
    total = shares[0].astype(F32)
    for i in range(1, shares.shape[0]):
        total = total + shares[i].astype(F32)
    out[...] = total.astype(out.dtype)


def spread_kernel(s0, s1, s2, s3, out):
    total = (s0[...].astype(F32) + s1[...].astype(F32)) + (
        s2[...].astype(F32) + s3[...].astype(F32)
    )
    err = total.astype(BF)
    for i in range(out.shape[0]):
        out[i] = err


def grad_kernel(flip, keep, err, dec, out):
    slab = dec[flip - 1] if flip else dec[...]
    term = lax.dot_general(err[...], slab, (((1,), (1,)), ((), ())), **DOT)
    out[...] = (keep[flip, 0:1, :] * term).astype(out.dtype)


def join_kernel(a, b, out):
    out[...] = (a[...] + b[...].astype(F32)).astype(out.dtype)


def turn_kernel(dec, out):
    for flip in (2, 3):
        out[flip - 2] = dec[flip - 1].T


def turned_kernel(flip, keep, err, turned, out):
    term = jnp.dot(err[...], turned[flip - 2], **DOT)
    out[...] = (keep[flip, 0:1, :] * term).astype(out.dtype)


def pick_kernel(err, out):
    base = spot_of() * out.shape[0]
    block = pl.multiple_of(base // 16 * 16, 16)
    value = err[pl.ds(block, 16), :].astype(F32)
    row_ids = lax.broadcasted_iota(jnp.int32, (16, 1), 0) + block
    for r in range(out.shape[0]):
        row = jnp.sum(jnp.where(row_ids == base + r, value, 0.0), axis=0, keepdims=True)
        out[r : r + 1, :] = row.astype(out.dtype)


def swap(value, name, flip):
    size = lax.axis_size(name)
    return lax.ppermute(value, name, [(i, i ^ flip) for i in range(size)])


def in_hbm(value):
    return pltpu.with_memory_space_constraint(value, pltpu.HBM)


def call(kernel, outs, specs, flops=0, moved=0, scratch=(), out_spec=VMEM):
    return pl.pallas_call(
        kernel,
        out_shape=outs,
        in_specs=specs,
        out_specs=out_spec,
        scratch_shapes=scratch,
        cost_estimate=cost(flops, moved),
        compiler_params=pltpu.CompilerParams(vmem_limit_bytes=LIMIT),
    )


def per_device(sources, targets, enc_weight, enc_bias, dec_weight, pair_mask):
    tok, width = sources.shape[1], sources.shape[2]
    feats = enc_weight.shape[2]
    rows_local = targets.shape[1]
    rows = tok // GROUP
    shape = jax.ShapeDtypeStruct

    chunks = 3
    slabs = in_hbm(dec_weight[0])
    latent, mine = call(
        encode_kernel,
        [shape((tok, feats), BF), shape((feats, width), BF)],
        [ANY] * 4,
        2 * tok * feats * width,
        2 * feats * width,
        scratch=[
            pltpu.VMEM((tok, width), BF),
            pltpu.VMEM((chunks, width // chunks, feats), BF),
            pltpu.VMEM((1, feats), F32),
            pltpu.SemaphoreType.DMA((chunks + 3,)),
        ],
        out_spec=[VMEM] * 2,
    )(in_hbm(sources[0]), in_hbm(enc_weight[0]), in_hbm(enc_bias), slabs)
    l2 = swap(latent, "tgt", 2)
    l1 = swap(latent, "tgt", 1)
    flops = 2 * tok * feats * width
    load = call(
        load_kernel,
        [
            shape((TG - 1, feats, width), BF),
            shape((tok, width), F32),
            shape((TG, 8, feats), F32),
        ],
        [ANY, VMEM, VMEM, ANY],
        flops,
        2 * TG * feats * width,
        scratch=[pltpu.SMEM((TG, TG), jnp.int32), pltpu.SemaphoreType.DMA((TG,))],
        out_spec=[VMEM] * 3,
    )
    dec, own, keep = load(in_hbm(pair_mask), latent, mine, slabs)
    l3 = swap(l2, "tgt", 1)
    most = call(decode_pair_kernel, shape((tok, width), F32), [VMEM] * 5, 2 * flops)(
        keep, own, l1, l2, dec
    )
    shares = call(decode_last_kernel, shape((tok, width), BF), [VMEM] * 5, flops)(
        keep, most, l3, targets[0], dec
    )

    shares = shares.reshape(GROUP, rows, width)
    shares = lax.all_to_all(shares, NEAR, 0, 0, tiled=True)
    near = call(gather_sum_kernel, shape((rows, width), BF), [VMEM])(shares)
    parts = [near] * ZH
    for flip in (2, 3, 1):
        parts[flip] = swap(near, "zh", flip)
    turned = call(turn_kernel, shape((2, width, feats), BF), [VMEM])(dec)
    copies = call(spread_kernel, shape((GROUP, rows, width), BF), [VMEM] * 4)(*parts)
    err_full = lax.all_to_all(copies, NEAR, 0, 0, tiled=True).reshape(tok, width)

    def term(flip, kind):
        far = flip > 1
        kernel = functools.partial(turned_kernel if far else grad_kernel, flip)
        slab = turned if far else dec if flip else mine
        return call(kernel, shape((tok, feats), kind), [VMEM] * 3, flops)(
            keep, err_full, slab
        )

    diag = term(3, BF)
    diag = swap(diag, "tgt", 1)
    far = term(2, F32)
    far = call(join_kernel, shape((tok, feats), BF), [VMEM] * 2)(far, diag)
    far = swap(far, "tgt", 2)
    near = term(1, BF)
    near = swap(near, "tgt", 1)
    grad = term(0, F32)
    err_local = call(pick_kernel, shape((rows_local, width), BF), [VMEM])(err_full)
    grad = grad + near.astype(F32) + far.astype(F32)
    return (err_local[None], grad.astype(BF)[None])


def solution(mesh):
    grid = Mesh(
        mesh.devices.reshape(X, YH, ZH, ZL, TG), ("x", "yh", "zh", "zl", "tgt")
    )
    in_specs = (
        P("tgt", None, None),
        P("tgt", FEAT, None),
        P("tgt", None, FEAT),
        P("tgt", FEAT),
        P("tgt", None, FEAT, None),
        P(),
    )
    out_specs = (P("tgt", FEAT, None), P("tgt", None, FEAT))
    return jax.shard_map(
        per_device, mesh=grid, in_specs=in_specs, out_specs=out_specs, check_vma=False
    )
```

```python
import functools

import jax
import jax.numpy as jnp
from jax import lax
from jax.experimental import pallas as pl
from jax.experimental.pallas import tpu as pltpu
from jax.sharding import Mesh, PartitionSpec as P


X, YH, ZH, ZL, TG = 4, 2, 4, 2, 4
NEAR = ("x", "yh", "zl")
FEAT = ("x", "yh", "zh", "zl")
GROUP = X * YH * ZL
DOT = dict(preferred_element_type=jnp.float32)
BF, F32 = jnp.bfloat16, jnp.float32
VMEM = pl.BlockSpec(memory_space=pltpu.VMEM)
ANY = pl.BlockSpec(memory_space=pl.ANY)
LIMIT = 24 * 1024 * 1024
FLIPS = (1, 2, 3)


def cost(flops, moved):
    return pl.CostEstimate(flops=flops, bytes_accessed=moved, transcendentals=0)


def spot_of():
    index = lax.axis_index("x")
    for name, size in (("yh", YH), ("zh", ZH), ("zl", ZL)):
        index = index * size + lax.axis_index(name)
    return index


def encode_kernel(sources, weight, bias, dec, latent, mine, src, wts, shift, sems):
    chunks = wts.shape[0]
    depth = wts.shape[1]
    copies = [pltpu.make_async_copy(sources, src, sems.at[chunks])]
    for i in range(chunks):
        part = weight.at[pl.ds(i * depth, depth), :]
        copies.append(pltpu.make_async_copy(part, wts.at[i], sems.at[i]))
    late = [
        pltpu.make_async_copy(bias, shift, sems.at[chunks + 1]),
        pltpu.make_async_copy(dec.at[lax.axis_index("tgt")], mine, sems.at[chunks + 2]),
    ]
    for copy in copies + late:
        copy.start()
    copies[0].wait()
    total = None
    for i in range(chunks):
        copies[i + 1].wait()
        part = jnp.dot(src[:, pl.ds(i * depth, depth)], wts[i], **DOT)
        total = part if total is None else total + part
    late[0].wait()
    latent[...] = jnp.maximum(total + shift[...], 0.0).astype(BF)
    late[1].wait()


def load_kernel(mask, latent, mine, dec, held, own, keep, flags, sems):
    owner = lax.axis_index("tgt")
    first = pltpu.make_async_copy(mask, flags, sems.at[0])
    first.start()
    copies = []
    for flip in FLIPS:
        peer = owner ^ flip
        copies.append(
            pltpu.make_async_copy(dec.at[peer], held.at[flip - 1], sems.at[flip])
        )
    for copy in copies:
        copy.start()
    first.wait()
    for flip in range(TG):
        value = flags[owner, owner ^ flip].astype(F32)
        keep[flip] = jnp.full(keep.shape[1:], value, F32)
    rows = latent[...] * keep[0, 0:1, :].astype(BF)
    own[...] = jnp.dot(rows, mine[...], **DOT)
    for copy in copies:
        copy.wait()


def decode_pair_kernel(keep, own, l1, l2, dec, out):
    step = 256
    rows = []
    for flip, ref in ((1, l1), (2, l2)):
        rows.append((flip - 1, ref[...] * keep[flip, 0:1, :].astype(BF)))
    for start in range(0, out.shape[1], step):
        cols = pl.ds(start, step)
        total = own[:, cols]
        for slab, latent in rows:
            total = total + jnp.dot(latent, dec[slab, :, cols], **DOT)
        out[:, cols] = total


def decode_last_kernel(keep, most, l3, targets, dec, out):
    base = spot_of() * targets.shape[0]
    tok, width = out.shape
    step = 256
    latent = l3[...] * keep[3, 0:1, :].astype(BF)
    row_ids = lax.broadcasted_iota(jnp.int32, (tok, 1), 0)
    for start in range(0, width, step):
        cols = pl.ds(start, step)
        total = most[:, cols] + jnp.dot(latent, dec[2, :, cols], **DOT)
        for r in range(targets.shape[0]):
            line = targets[r : r + 1, cols].astype(F32)
            total = total - jnp.where(row_ids == base + r, line, 0.0)
        out[:, cols] = total.astype(BF)


def gather_sum_kernel(shares, out):
    total = shares[0].astype(F32)
    for i in range(1, shares.shape[0]):
        total = total + shares[i].astype(F32)
    out[...] = total.astype(out.dtype)


def spread_kernel(s0, s1, s2, s3, out):
    total = (s0[...].astype(F32) + s1[...].astype(F32)) + (
        s2[...].astype(F32) + s3[...].astype(F32)
    )
    err = total.astype(BF)
    for i in range(out.shape[0]):
        out[i] = err


def join_kernel(a, b, out):
    out[...] = (a[...] + b[...].astype(F32)).astype(out.dtype)


def turn_kernel(mine, dec, out):
    out[0] = mine[...].T
    for flip in FLIPS:
        out[flip] = dec[flip - 1].T


def term_kernel(flip, keep, err, turned, out):
    term = jnp.dot(err[...], turned[flip], **DOT)
    out[...] = (keep[flip, 0:1, :] * term).astype(out.dtype)


def pick_kernel(err, out):
    base = spot_of() * out.shape[0]
    block = pl.multiple_of(base // 16 * 16, 16)
    value = err[pl.ds(block, 16), :].astype(F32)
    row_ids = lax.broadcasted_iota(jnp.int32, (16, 1), 0) + block
    for r in range(out.shape[0]):
        row = jnp.sum(jnp.where(row_ids == base + r, value, 0.0), axis=0, keepdims=True)
        out[r : r + 1, :] = row.astype(out.dtype)


def swap(value, name, flip):
    size = lax.axis_size(name)
    return lax.ppermute(value, name, [(i, i ^ flip) for i in range(size)])


def in_hbm(value):
    return pltpu.with_memory_space_constraint(value, pltpu.HBM)


def call(kernel, outs, specs, flops=0, moved=0, scratch=(), out_spec=VMEM):
    return pl.pallas_call(
        kernel,
        out_shape=outs,
        in_specs=specs,
        out_specs=out_spec,
        scratch_shapes=scratch,
        cost_estimate=cost(flops, moved),
        compiler_params=pltpu.CompilerParams(vmem_limit_bytes=LIMIT),
    )


def per_device(sources, targets, enc_weight, enc_bias, dec_weight, pair_mask):
    tok, width = sources.shape[1], sources.shape[2]
    feats = enc_weight.shape[2]
    rows_local = targets.shape[1]
    rows = tok // GROUP
    shape = jax.ShapeDtypeStruct

    chunks = 3
    slabs = in_hbm(dec_weight[0])
    latent, mine = call(
        encode_kernel,
        [shape((tok, feats), BF), shape((feats, width), BF)],
        [ANY] * 4,
        2 * tok * feats * width,
        2 * feats * width,
        scratch=[
            pltpu.VMEM((tok, width), BF),
            pltpu.VMEM((chunks, width // chunks, feats), BF),
            pltpu.VMEM((1, feats), F32),
            pltpu.SemaphoreType.DMA((chunks + 3,)),
        ],
        out_spec=[VMEM] * 2,
    )(in_hbm(sources[0]), in_hbm(enc_weight[0]), in_hbm(enc_bias), slabs)
    l2 = swap(latent, "tgt", 2)
    l1 = swap(latent, "tgt", 1)
    flops = 2 * tok * feats * width
    load = call(
        load_kernel,
        [
            shape((TG - 1, feats, width), BF),
            shape((tok, width), F32),
            shape((TG, 8, feats), F32),
        ],
        [ANY, VMEM, VMEM, ANY],
        flops,
        2 * TG * feats * width,
        scratch=[pltpu.SMEM((TG, TG), jnp.int32), pltpu.SemaphoreType.DMA((TG,))],
        out_spec=[VMEM] * 3,
    )
    dec, own, keep = load(in_hbm(pair_mask), latent, mine, slabs)
    l3 = swap(l2, "tgt", 1)
    most = call(decode_pair_kernel, shape((tok, width), F32), [VMEM] * 5, 2 * flops)(
        keep, own, l1, l2, dec
    )
    shares = call(decode_last_kernel, shape((tok, width), BF), [VMEM] * 5, flops)(
        keep, most, l3, targets[0], dec
    )

    shares = shares.reshape(GROUP, rows, width)
    shares = lax.all_to_all(shares, NEAR, 0, 0, tiled=True)
    near = call(gather_sum_kernel, shape((rows, width), BF), [VMEM])(shares)
    parts = [near] * ZH
    for flip in (2, 3, 1):
        parts[flip] = swap(near, "zh", flip)
    turned = call(turn_kernel, shape((TG, width, feats), BF), [VMEM] * 2)(mine, dec)
    copies = call(spread_kernel, shape((GROUP, rows, width), BF), [VMEM] * 4)(*parts)
    err_full = lax.all_to_all(copies, NEAR, 0, 0, tiled=True).reshape(tok, width)

    def term(flip, kind):
        kernel = functools.partial(term_kernel, flip)
        return call(kernel, shape((tok, feats), kind), [VMEM] * 3, flops)(
            keep, err_full, turned
        )

    diag = term(3, BF)
    diag = swap(diag, "tgt", 1)
    far = term(2, F32)
    far = call(join_kernel, shape((tok, feats), BF), [VMEM] * 2)(far, diag)
    far = swap(far, "tgt", 2)
    near = term(1, BF)
    near = swap(near, "tgt", 1)
    grad = term(0, F32)
    err_local = call(pick_kernel, shape((rows_local, width), BF), [VMEM])(err_full)
    grad = grad + near.astype(F32) + far.astype(F32)
    return (err_local[None], grad.astype(BF)[None])


def solution(mesh):
    grid = Mesh(
        mesh.devices.reshape(X, YH, ZH, ZL, TG), ("x", "yh", "zh", "zl", "tgt")
    )
    in_specs = (
        P("tgt", None, None),
        P("tgt", FEAT, None),
        P("tgt", None, FEAT),
        P("tgt", FEAT),
        P("tgt", None, FEAT, None),
        P(),
    )
    out_specs = (P("tgt", FEAT, None), P("tgt", None, FEAT))
    return jax.shard_map(
        per_device, mesh=grid, in_specs=in_specs, out_specs=out_specs, check_vma=False
    )
```

```python
import functools

import jax
import jax.numpy as jnp
from jax import lax
from jax.experimental import pallas as pl
from jax.experimental.pallas import tpu as pltpu
from jax.sharding import Mesh, PartitionSpec as P


X, YH, ZH, ZL, TG = 4, 2, 4, 2, 4
NEAR = ("x", "yh", "zl")
FEAT = ("x", "yh", "zh", "zl")
GROUP = X * YH * ZL
DOT = dict(preferred_element_type=jnp.float32)
BF, F32 = jnp.bfloat16, jnp.float32
VMEM = pl.BlockSpec(memory_space=pltpu.VMEM)
ANY = pl.BlockSpec(memory_space=pl.ANY)
LIMIT = 24 * 1024 * 1024
FLIPS = (1, 2, 3)


def cost(flops, moved):
    return pl.CostEstimate(flops=flops, bytes_accessed=moved, transcendentals=0)


def spot_of():
    index = lax.axis_index("x")
    for name, size in (("yh", YH), ("zh", ZH), ("zl", ZL)):
        index = index * size + lax.axis_index(name)
    return index


def encode_kernel(sources, weight, bias, dec, latent, mine, src, wts, shift, sems):
    chunks = wts.shape[0]
    depth = wts.shape[1]
    copies = [pltpu.make_async_copy(sources, src, sems.at[chunks])]
    for i in range(chunks):
        part = weight.at[pl.ds(i * depth, depth), :]
        copies.append(pltpu.make_async_copy(part, wts.at[i], sems.at[i]))
    late = [
        pltpu.make_async_copy(bias, shift, sems.at[chunks + 1]),
        pltpu.make_async_copy(dec.at[lax.axis_index("tgt")], mine, sems.at[chunks + 2]),
    ]
    for copy in copies + late:
        copy.start()
    copies[0].wait()
    total = None
    for i in range(chunks):
        copies[i + 1].wait()
        part = jnp.dot(src[:, pl.ds(i * depth, depth)], wts[i], **DOT)
        total = part if total is None else total + part
    late[0].wait()
    latent[...] = jnp.maximum(total + shift[...], 0.0).astype(BF)
    late[1].wait()


def load_kernel(mask, latent, mine, dec, held, own, keep, flags, sems):
    owner = lax.axis_index("tgt")
    first = pltpu.make_async_copy(mask, flags, sems.at[0])
    first.start()
    copies = []
    for flip in FLIPS:
        peer = owner ^ flip
        copies.append(
            pltpu.make_async_copy(dec.at[peer], held.at[flip - 1], sems.at[flip])
        )
    for copy in copies:
        copy.start()
    first.wait()
    for flip in range(TG):
        value = flags[owner, owner ^ flip].astype(F32)
        keep[flip] = jnp.full(keep.shape[1:], value, F32)
    rows = latent[...] * keep[0, 0:1, :].astype(BF)
    own[...] = jnp.dot(rows, mine[...], **DOT)
    for copy in copies:
        copy.wait()


def decode_pair_kernel(keep, own, l1, l2, dec, out):
    step = 256
    rows = []
    for flip, ref in ((1, l1), (2, l2)):
        rows.append((flip - 1, ref[...] * keep[flip, 0:1, :].astype(BF)))
    for start in range(0, out.shape[1], step):
        cols = pl.ds(start, step)
        total = own[:, cols]
        for slab, latent in rows:
            total = total + jnp.dot(latent, dec[slab, :, cols], **DOT)
        out[:, cols] = total


def decode_last_kernel(keep, most, l3, targets, mine, dec, out, turned):
    base = spot_of() * targets.shape[0]
    tok, width = out.shape
    step = 256
    latent = l3[...] * keep[3, 0:1, :].astype(BF)
    row_ids = lax.broadcasted_iota(jnp.int32, (tok, 1), 0)
    for start in range(0, width, step):
        cols = pl.ds(start, step)
        total = most[:, cols] + jnp.dot(latent, dec[2, :, cols], **DOT)
        for r in range(targets.shape[0]):
            line = targets[r : r + 1, cols].astype(F32)
            total = total - jnp.where(row_ids == base + r, line, 0.0)
        out[:, cols] = total.astype(BF)

    @pl.when(lax.axis_index("tgt") % 2 == 1)
    def _():
        turn(mine, dec, turned)


def gather_sum_kernel(shares, out):
    total = shares[0].astype(F32)
    for i in range(1, shares.shape[0]):
        total = total + shares[i].astype(F32)
    out[...] = total.astype(out.dtype)


def spread_kernel(s0, s1, s2, s3, out):
    total = (s0[...].astype(F32) + s1[...].astype(F32)) + (
        s2[...].astype(F32) + s3[...].astype(F32)
    )
    err = total.astype(BF)
    for i in range(out.shape[0]):
        out[i] = err


def join_kernel(a, b, out):
    out[...] = (a[...] + b[...].astype(F32)).astype(out.dtype)


def turn(mine, dec, out):
    out[0] = mine[...].T
    for flip in FLIPS:
        out[flip] = dec[flip - 1].T


def turn_kernel(mine, dec, early, out):
    @pl.when(lax.axis_index("tgt") % 2 == 0)
    def _():
        turn(mine, dec, out)


def term_kernel(flip, keep, err, turned, out):
    term = jnp.dot(err[...], turned[flip], **DOT)
    out[...] = (keep[flip, 0:1, :] * term).astype(out.dtype)


def pick_kernel(err, out):
    base = spot_of() * out.shape[0]
    block = pl.multiple_of(base // 16 * 16, 16)
    value = err[pl.ds(block, 16), :].astype(F32)
    row_ids = lax.broadcasted_iota(jnp.int32, (16, 1), 0) + block
    for r in range(out.shape[0]):
        row = jnp.sum(jnp.where(row_ids == base + r, value, 0.0), axis=0, keepdims=True)
        out[r : r + 1, :] = row.astype(out.dtype)


def swap(value, name, flip):
    size = lax.axis_size(name)
    return lax.ppermute(value, name, [(i, i ^ flip) for i in range(size)])


def in_hbm(value):
    return pltpu.with_memory_space_constraint(value, pltpu.HBM)


def call(kernel, outs, specs, flops=0, moved=0, scratch=(), out_spec=VMEM, alias=None):
    return pl.pallas_call(
        kernel,
        out_shape=outs,
        in_specs=specs,
        out_specs=out_spec,
        scratch_shapes=scratch,
        input_output_aliases=alias or {},
        cost_estimate=cost(flops, moved),
        compiler_params=pltpu.CompilerParams(vmem_limit_bytes=LIMIT),
    )


def per_device(sources, targets, enc_weight, enc_bias, dec_weight, pair_mask):
    tok, width = sources.shape[1], sources.shape[2]
    feats = enc_weight.shape[2]
    rows_local = targets.shape[1]
    rows = tok // GROUP
    shape = jax.ShapeDtypeStruct

    chunks = 3
    slabs = in_hbm(dec_weight[0])
    latent, mine = call(
        encode_kernel,
        [shape((tok, feats), BF), shape((feats, width), BF)],
        [ANY] * 4,
        2 * tok * feats * width,
        2 * feats * width,
        scratch=[
            pltpu.VMEM((tok, width), BF),
            pltpu.VMEM((chunks, width // chunks, feats), BF),
            pltpu.VMEM((1, feats), F32),
            pltpu.SemaphoreType.DMA((chunks + 3,)),
        ],
        out_spec=[VMEM] * 2,
    )(in_hbm(sources[0]), in_hbm(enc_weight[0]), in_hbm(enc_bias), slabs)
    l2 = swap(latent, "tgt", 2)
    l1 = swap(latent, "tgt", 1)
    flops = 2 * tok * feats * width
    load = call(
        load_kernel,
        [
            shape((TG - 1, feats, width), BF),
            shape((tok, width), F32),
            shape((TG, 8, feats), F32),
        ],
        [ANY, VMEM, VMEM, ANY],
        flops,
        2 * TG * feats * width,
        scratch=[pltpu.SMEM((TG, TG), jnp.int32), pltpu.SemaphoreType.DMA((TG,))],
        out_spec=[VMEM] * 3,
    )
    dec, own, keep = load(in_hbm(pair_mask), latent, mine, slabs)
    l3 = swap(l2, "tgt", 1)
    most = call(decode_pair_kernel, shape((tok, width), F32), [VMEM] * 5, 2 * flops)(
        keep, own, l1, l2, dec
    )
    turns = shape((TG, width, feats), BF)
    shares, early = call(
        decode_last_kernel,
        [shape((tok, width), BF), turns],
        [VMEM] * 6,
        flops,
        out_spec=[VMEM] * 2,
    )(keep, most, l3, targets[0], mine, dec)

    shares = shares.reshape(GROUP, rows, width)
    shares = lax.all_to_all(shares, NEAR, 0, 0, tiled=True)
    near = call(gather_sum_kernel, shape((rows, width), BF), [VMEM])(shares)
    parts = [near] * ZH
    for flip in (2, 3, 1):
        parts[flip] = swap(near, "zh", flip)
    turned = call(turn_kernel, turns, [VMEM, VMEM, ANY], alias={2: 0})(mine, dec, early)
    copies = call(spread_kernel, shape((GROUP, rows, width), BF), [VMEM] * 4)(*parts)
    err_full = lax.all_to_all(copies, NEAR, 0, 0, tiled=True).reshape(tok, width)

    def term(flip, kind):
        kernel = functools.partial(term_kernel, flip)
        return call(kernel, shape((tok, feats), kind), [VMEM] * 3, flops)(
            keep, err_full, turned
        )

    diag = term(3, BF)
    diag = swap(diag, "tgt", 1)
    far = term(2, F32)
    far = call(join_kernel, shape((tok, feats), BF), [VMEM] * 2)(far, diag)
    far = swap(far, "tgt", 2)
    near = term(1, BF)
    near = swap(near, "tgt", 1)
    grad = term(0, F32)
    err_local = call(pick_kernel, shape((rows_local, width), BF), [VMEM])(err_full)
    grad = grad + near.astype(F32) + far.astype(F32)
    return (err_local[None], grad.astype(BF)[None])


def solution(mesh):
    grid = Mesh(
        mesh.devices.reshape(X, YH, ZH, ZL, TG), ("x", "yh", "zh", "zl", "tgt")
    )
    in_specs = (
        P("tgt", None, None),
        P("tgt", FEAT, None),
        P("tgt", None, FEAT),
        P("tgt", FEAT),
        P("tgt", None, FEAT, None),
        P(),
    )
    out_specs = (P("tgt", FEAT, None), P("tgt", None, FEAT))
    return jax.shard_map(
        per_device, mesh=grid, in_specs=in_specs, out_specs=out_specs, check_vma=False
    )
```

```python
import functools

import jax
import jax.numpy as jnp
from jax import lax
from jax.experimental import pallas as pl
from jax.experimental.pallas import tpu as pltpu
from jax.sharding import Mesh, PartitionSpec as P


X, YH, ZH, ZL, TG = 4, 2, 4, 2, 4
NEAR = ("x", "yh", "zl")
FEAT = ("x", "yh", "zh", "zl")
GROUP = X * YH * ZL
DOT = dict(preferred_element_type=jnp.float32)
BF, F32 = jnp.bfloat16, jnp.float32
VMEM = pl.BlockSpec(memory_space=pltpu.VMEM)
ANY = pl.BlockSpec(memory_space=pl.ANY)
LIMIT = 24 * 1024 * 1024
FLIPS = (1, 2, 3)


def cost(flops, moved):
    return pl.CostEstimate(flops=flops, bytes_accessed=moved, transcendentals=0)


def spot_of():
    index = lax.axis_index("x")
    for name, size in (("yh", YH), ("zh", ZH), ("zl", ZL)):
        index = index * size + lax.axis_index(name)
    return index


def encode_kernel(sources, weight, bias, dec, latent, mine, src, wts, shift, sems):
    chunks = wts.shape[0]
    depth = wts.shape[1]
    copies = [pltpu.make_async_copy(sources, src, sems.at[chunks])]
    for i in range(chunks):
        part = weight.at[pl.ds(i * depth, depth), :]
        copies.append(pltpu.make_async_copy(part, wts.at[i], sems.at[i]))
    late = [
        pltpu.make_async_copy(bias, shift, sems.at[chunks + 1]),
        pltpu.make_async_copy(dec.at[lax.axis_index("tgt")], mine, sems.at[chunks + 2]),
    ]
    for copy in copies + late:
        copy.start()
    copies[0].wait()
    total = None
    for i in range(chunks):
        copies[i + 1].wait()
        part = jnp.dot(src[:, pl.ds(i * depth, depth)], wts[i], **DOT)
        total = part if total is None else total + part
    late[0].wait()
    latent[...] = jnp.maximum(total + shift[...], 0.0).astype(BF)
    late[1].wait()


def load_kernel(mask, latent, mine, dec, held, own, keep, flags, sems):
    owner = lax.axis_index("tgt")
    first = pltpu.make_async_copy(mask, flags, sems.at[0])
    first.start()
    copies = []
    for flip in FLIPS:
        peer = owner ^ flip
        copies.append(
            pltpu.make_async_copy(dec.at[peer], held.at[flip - 1], sems.at[flip])
        )
    for copy in copies:
        copy.start()
    first.wait()
    for flip in range(TG):
        value = flags[owner, owner ^ flip].astype(F32)
        keep[flip] = jnp.full(keep.shape[1:], value, F32)
    rows = latent[...] * keep[0, 0:1, :].astype(BF)
    own[...] = jnp.dot(rows, mine[...], **DOT)
    for copy in copies:
        copy.wait()


def decode_pair_kernel(keep, own, l1, l2, targets, dec, out):
    base = spot_of() * targets.shape[0]
    tok, width = out.shape
    step = 256
    rows = []
    for flip, ref in ((1, l1), (2, l2)):
        rows.append((flip - 1, ref[...] * keep[flip, 0:1, :].astype(BF)))
    row_ids = lax.broadcasted_iota(jnp.int32, (tok, 1), 0)
    for start in range(0, width, step):
        cols = pl.ds(start, step)
        total = own[:, cols]
        for slab, latent in rows:
            total = total + jnp.dot(latent, dec[slab, :, cols], **DOT)
        for r in range(targets.shape[0]):
            line = targets[r : r + 1, cols].astype(F32)
            total = total - jnp.where(row_ids == base + r, line, 0.0)
        out[:, cols] = total


def decode_last_kernel(keep, most, l3, dec, out):
    step = 256
    latent = l3[...] * keep[3, 0:1, :].astype(BF)
    for start in range(0, out.shape[1], step):
        cols = pl.ds(start, step)
        total = most[:, cols] + jnp.dot(latent, dec[2, :, cols], **DOT)
        out[:, cols] = total.astype(BF)


def gather_sum_kernel(shares, out):
    total = shares[0].astype(F32)
    for i in range(1, shares.shape[0]):
        total = total + shares[i].astype(F32)
    out[...] = total.astype(out.dtype)


def spread_kernel(s0, s1, s2, s3, out):
    total = (s0[...].astype(F32) + s1[...].astype(F32)) + (
        s2[...].astype(F32) + s3[...].astype(F32)
    )
    err = total.astype(BF)
    for i in range(out.shape[0]):
        out[i] = err


def join_kernel(a, b, out):
    out[...] = (a[...] + b[...].astype(F32)).astype(out.dtype)


def turn_kernel(mine, dec, out):
    out[0] = mine[...].T
    for flip in FLIPS:
        out[flip] = dec[flip - 1].T


def term_kernel(flip, keep, err, turned, out):
    term = jnp.dot(err[...], turned[flip], **DOT)
    out[...] = (keep[flip, 0:1, :] * term).astype(out.dtype)


def pick_kernel(err, out):
    base = spot_of() * out.shape[0]
    block = pl.multiple_of(base // 16 * 16, 16)
    value = err[pl.ds(block, 16), :].astype(F32)
    row_ids = lax.broadcasted_iota(jnp.int32, (16, 1), 0) + block
    for r in range(out.shape[0]):
        row = jnp.sum(jnp.where(row_ids == base + r, value, 0.0), axis=0, keepdims=True)
        out[r : r + 1, :] = row.astype(out.dtype)


def swap(value, name, flip):
    size = lax.axis_size(name)
    return lax.ppermute(value, name, [(i, i ^ flip) for i in range(size)])


def in_hbm(value):
    return pltpu.with_memory_space_constraint(value, pltpu.HBM)


def call(kernel, outs, specs, flops=0, moved=0, scratch=(), out_spec=VMEM):
    return pl.pallas_call(
        kernel,
        out_shape=outs,
        in_specs=specs,
        out_specs=out_spec,
        scratch_shapes=scratch,
        cost_estimate=cost(flops, moved),
        compiler_params=pltpu.CompilerParams(vmem_limit_bytes=LIMIT),
    )


def per_device(sources, targets, enc_weight, enc_bias, dec_weight, pair_mask):
    tok, width = sources.shape[1], sources.shape[2]
    feats = enc_weight.shape[2]
    rows_local = targets.shape[1]
    rows = tok // GROUP
    shape = jax.ShapeDtypeStruct

    chunks = 3
    slabs = in_hbm(dec_weight[0])
    latent, mine = call(
        encode_kernel,
        [shape((tok, feats), BF), shape((feats, width), BF)],
        [ANY] * 4,
        2 * tok * feats * width,
        2 * feats * width,
        scratch=[
            pltpu.VMEM((tok, width), BF),
            pltpu.VMEM((chunks, width // chunks, feats), BF),
            pltpu.VMEM((1, feats), F32),
            pltpu.SemaphoreType.DMA((chunks + 3,)),
        ],
        out_spec=[VMEM] * 2,
    )(in_hbm(sources[0]), in_hbm(enc_weight[0]), in_hbm(enc_bias), slabs)
    l2 = swap(latent, "tgt", 2)
    l1 = swap(latent, "tgt", 1)
    flops = 2 * tok * feats * width
    load = call(
        load_kernel,
        [
            shape((TG - 1, feats, width), BF),
            shape((tok, width), F32),
            shape((TG, 8, feats), F32),
        ],
        [ANY, VMEM, VMEM, ANY],
        flops,
        2 * TG * feats * width,
        scratch=[pltpu.SMEM((TG, TG), jnp.int32), pltpu.SemaphoreType.DMA((TG,))],
        out_spec=[VMEM] * 3,
    )
    dec, own, keep = load(in_hbm(pair_mask), latent, mine, slabs)
    l3 = swap(l2, "tgt", 1)
    most = call(decode_pair_kernel, shape((tok, width), F32), [VMEM] * 6, 2 * flops)(
        keep, own, l1, l2, targets[0], dec
    )
    shares = call(decode_last_kernel, shape((tok, width), BF), [VMEM] * 4, flops)(
        keep, most, l3, dec
    )

    shares = shares.reshape(GROUP, rows, width)
    shares = lax.all_to_all(shares, NEAR, 0, 0, tiled=True)
    near = call(gather_sum_kernel, shape((rows, width), BF), [VMEM])(shares)
    parts = [near] * ZH
    for flip in (2, 3, 1):
        parts[flip] = swap(near, "zh", flip)
    turned = call(turn_kernel, shape((TG, width, feats), BF), [VMEM] * 2)(mine, dec)
    copies = call(spread_kernel, shape((GROUP, rows, width), BF), [VMEM] * 4)(*parts)
    err_full = lax.all_to_all(copies, NEAR, 0, 0, tiled=True).reshape(tok, width)

    def term(flip, kind):
        kernel = functools.partial(term_kernel, flip)
        return call(kernel, shape((tok, feats), kind), [VMEM] * 3, flops)(
            keep, err_full, turned
        )

    diag = term(3, BF)
    diag = swap(diag, "tgt", 1)
    far = term(2, F32)
    far = call(join_kernel, shape((tok, feats), BF), [VMEM] * 2)(far, diag)
    far = swap(far, "tgt", 2)
    near = term(1, BF)
    near = swap(near, "tgt", 1)
    grad = term(0, F32)
    err_local = call(pick_kernel, shape((rows_local, width), BF), [VMEM])(err_full)
    grad = grad + near.astype(F32) + far.astype(F32)
    return (err_local[None], grad.astype(BF)[None])


def solution(mesh):
    grid = Mesh(
        mesh.devices.reshape(X, YH, ZH, ZL, TG), ("x", "yh", "zh", "zl", "tgt")
    )
    in_specs = (
        P("tgt", None, None),
        P("tgt", FEAT, None),
        P("tgt", None, FEAT),
        P("tgt", FEAT),
        P("tgt", None, FEAT, None),
        P(),
    )
    out_specs = (P("tgt", FEAT, None), P("tgt", None, FEAT))
    return jax.shard_map(
        per_device, mesh=grid, in_specs=in_specs, out_specs=out_specs, check_vma=False
    )
```

```python
import functools

import jax
import jax.numpy as jnp
from jax import lax
from jax.experimental import pallas as pl
from jax.experimental.pallas import tpu as pltpu
from jax.sharding import Mesh, PartitionSpec as P


X, YH, ZH, ZL, TG = 4, 2, 4, 2, 4
NEAR = ("x", "yh", "zl")
FEAT = ("x", "yh", "zh", "zl")
GROUP = X * YH * ZL
DOT = dict(preferred_element_type=jnp.float32)
BF, F32 = jnp.bfloat16, jnp.float32
VMEM = pl.BlockSpec(memory_space=pltpu.VMEM)
ANY = pl.BlockSpec(memory_space=pl.ANY)
LIMIT = 24 * 1024 * 1024
FLIPS = (1, 2, 3)


def cost(flops, moved):
    return pl.CostEstimate(flops=flops, bytes_accessed=moved, transcendentals=0)


def spot_of():
    index = lax.axis_index("x")
    for name, size in (("yh", YH), ("zh", ZH), ("zl", ZL)):
        index = index * size + lax.axis_index(name)
    return index


def encode_kernel(sources, weight, bias, dec, latent, mine, src, wts, shift, sems):
    chunks = wts.shape[0]
    depth = wts.shape[1]
    copies = [pltpu.make_async_copy(sources, src, sems.at[chunks])]
    for i in range(chunks):
        part = weight.at[pl.ds(i * depth, depth), :]
        copies.append(pltpu.make_async_copy(part, wts.at[i], sems.at[i]))
    late = [
        pltpu.make_async_copy(bias, shift, sems.at[chunks + 1]),
        pltpu.make_async_copy(dec.at[lax.axis_index("tgt")], mine, sems.at[chunks + 2]),
    ]
    for copy in copies + late:
        copy.start()
    copies[0].wait()
    total = None
    for i in range(chunks):
        copies[i + 1].wait()
        part = jnp.dot(src[:, pl.ds(i * depth, depth)], wts[i], **DOT)
        total = part if total is None else total + part
    late[0].wait()
    latent[...] = jnp.maximum(total + shift[...], 0.0).astype(BF)
    late[1].wait()


def load_kernel(mask, latent, mine, dec, held, own, keep, flags, sems):
    owner = lax.axis_index("tgt")
    first = pltpu.make_async_copy(mask, flags, sems.at[0])
    first.start()
    copies = []
    for flip in FLIPS:
        peer = owner ^ flip
        copies.append(
            pltpu.make_async_copy(dec.at[peer], held.at[flip - 1], sems.at[flip])
        )
    for copy in copies:
        copy.start()
    first.wait()
    for flip in range(TG):
        value = flags[owner, owner ^ flip].astype(F32)
        keep[flip] = jnp.full(keep.shape[1:], value, F32)
    rows = latent[...] * keep[0, 0:1, :].astype(BF)
    own[...] = jnp.dot(rows, mine[...], **DOT)
    for copy in copies:
        copy.wait()


def decode_pair_kernel(keep, own, l1, l2, targets, dec, out):
    base = spot_of() * targets.shape[0]
    tok, width = out.shape
    step = 256
    rows = []
    for flip, ref in ((1, l1), (2, l2)):
        rows.append((flip - 1, ref[...] * keep[flip, 0:1, :].astype(BF)))
    row_ids = lax.broadcasted_iota(jnp.int32, (tok, 1), 0)
    for start in range(0, width, step):
        cols = pl.ds(start, step)
        total = own[:, cols]
        for slab, latent in rows:
            total = total + jnp.dot(latent, dec[slab, :, cols], **DOT)
        for r in range(targets.shape[0]):
            line = targets[r : r + 1, cols].astype(F32)
            total = total - jnp.where(row_ids == base + r, line, 0.0)
        out[:, cols] = total


def decode_last_kernel(keep, most, l3, dec, out):
    step = 256
    latent = l3[...] * keep[3, 0:1, :].astype(BF)
    for start in range(0, out.shape[1], step):
        cols = pl.ds(start, step)
        total = most[:, cols] + jnp.dot(latent, dec[2, :, cols], **DOT)
        out[:, cols] = total.astype(BF)


def gather_sum_kernel(shares, out):
    total = shares[0].astype(F32)
    for i in range(1, shares.shape[0]):
        total = total + shares[i].astype(F32)
    value = total.astype(out.dtype)
    for i in range(out.shape[0]):
        out[i] = value


def spread_kernel(parts, out):
    total = (parts[0].astype(F32) + parts[1].astype(F32)) + (
        parts[2].astype(F32) + parts[3].astype(F32)
    )
    err = total.astype(BF)
    for i in range(out.shape[0]):
        out[i] = err


def join_kernel(a, b, out):
    out[...] = (a[...] + b[...].astype(F32)).astype(out.dtype)


def term_kernel(flip, keep, err, dec, out):
    slab = dec[flip - 1] if flip else dec[...]
    term = lax.dot_general(err[...], slab, (((1,), (1,)), ((), ())), **DOT)
    out[...] = (keep[flip, 0:1, :] * term).astype(out.dtype)


def pick_kernel(err, out):
    base = spot_of() * out.shape[0]
    block = pl.multiple_of(base // 16 * 16, 16)
    value = err[pl.ds(block, 16), :].astype(F32)
    row_ids = lax.broadcasted_iota(jnp.int32, (16, 1), 0) + block
    for r in range(out.shape[0]):
        row = jnp.sum(jnp.where(row_ids == base + r, value, 0.0), axis=0, keepdims=True)
        out[r : r + 1, :] = row.astype(out.dtype)


def swap(value, name, flip):
    size = lax.axis_size(name)
    return lax.ppermute(value, name, [(i, i ^ flip) for i in range(size)])


def in_hbm(value):
    return pltpu.with_memory_space_constraint(value, pltpu.HBM)


def call(kernel, outs, specs, flops=0, moved=0, scratch=(), out_spec=VMEM):
    return pl.pallas_call(
        kernel,
        out_shape=outs,
        in_specs=specs,
        out_specs=out_spec,
        scratch_shapes=scratch,
        cost_estimate=cost(flops, moved),
        compiler_params=pltpu.CompilerParams(vmem_limit_bytes=LIMIT),
    )


def per_device(sources, targets, enc_weight, enc_bias, dec_weight, pair_mask):
    tok, width = sources.shape[1], sources.shape[2]
    feats = enc_weight.shape[2]
    rows_local = targets.shape[1]
    rows = tok // GROUP
    shape = jax.ShapeDtypeStruct

    chunks = 3
    slabs = in_hbm(dec_weight[0])
    latent, mine = call(
        encode_kernel,
        [shape((tok, feats), BF), shape((feats, width), BF)],
        [ANY] * 4,
        2 * tok * feats * width,
        2 * feats * width,
        scratch=[
            pltpu.VMEM((tok, width), BF),
            pltpu.VMEM((chunks, width // chunks, feats), BF),
            pltpu.VMEM((1, feats), F32),
            pltpu.SemaphoreType.DMA((chunks + 3,)),
        ],
        out_spec=[VMEM] * 2,
    )(in_hbm(sources[0]), in_hbm(enc_weight[0]), in_hbm(enc_bias), slabs)
    l2 = swap(latent, "tgt", 2)
    l1 = swap(latent, "tgt", 1)
    flops = 2 * tok * feats * width
    load = call(
        load_kernel,
        [
            shape((TG - 1, feats, width), BF),
            shape((tok, width), F32),
            shape((TG, 8, feats), F32),
        ],
        [ANY, VMEM, VMEM, ANY],
        flops,
        2 * TG * feats * width,
        scratch=[pltpu.SMEM((TG, TG), jnp.int32), pltpu.SemaphoreType.DMA((TG,))],
        out_spec=[VMEM] * 3,
    )
    dec, own, keep = load(in_hbm(pair_mask), latent, mine, slabs)
    l3 = swap(l2, "tgt", 1)
    most = call(decode_pair_kernel, shape((tok, width), F32), [VMEM] * 6, 2 * flops)(
        keep, own, l1, l2, targets[0], dec
    )
    shares = call(decode_last_kernel, shape((tok, width), BF), [VMEM] * 4, flops)(
        keep, most, l3, dec
    )

    shares = shares.reshape(GROUP, rows, width)
    shares = lax.all_to_all(shares, NEAR, 0, 0, tiled=True)
    near = call(gather_sum_kernel, shape((ZH, rows, width), BF), [VMEM])(shares)
    parts = lax.all_to_all(near, "zh", 0, 0, tiled=True)
    copies = call(spread_kernel, shape((GROUP, rows, width), BF), [VMEM])(parts)
    err_full = lax.all_to_all(copies, NEAR, 0, 0, tiled=True).reshape(tok, width)

    def term(flip, kind):
        kernel = functools.partial(term_kernel, flip)
        return call(kernel, shape((tok, feats), kind), [VMEM] * 3, flops)(
            keep, err_full, dec if flip else mine
        )

    diag = term(3, BF)
    diag = swap(diag, "tgt", 1)
    far = term(2, F32)
    far = call(join_kernel, shape((tok, feats), BF), [VMEM] * 2)(far, diag)
    far = swap(far, "tgt", 2)
    near = term(1, BF)
    near = swap(near, "tgt", 1)
    grad = term(0, F32)
    err_local = call(pick_kernel, shape((rows_local, width), BF), [VMEM])(err_full)
    grad = grad + near.astype(F32) + far.astype(F32)
    return (err_local[None], grad.astype(BF)[None])


def solution(mesh):
    grid = Mesh(
        mesh.devices.reshape(X, YH, ZH, ZL, TG), ("x", "yh", "zh", "zl", "tgt")
    )
    in_specs = (
        P("tgt", None, None),
        P("tgt", FEAT, None),
        P("tgt", None, FEAT),
        P("tgt", FEAT),
        P("tgt", None, FEAT, None),
        P(),
    )
    out_specs = (P("tgt", FEAT, None), P("tgt", None, FEAT))
    return jax.shard_map(
        per_device, mesh=grid, in_specs=in_specs, out_specs=out_specs, check_vma=False
    )
```

```python
import functools

import jax
import jax.numpy as jnp
from jax import lax
from jax.experimental import pallas as pl
from jax.experimental.pallas import tpu as pltpu
from jax.sharding import Mesh, PartitionSpec as P


X, YH, ZH, ZL, TG = 4, 2, 4, 2, 4
NEAR = ("x", "zl")
FEAT = ("x", "yh", "zh", "zl")
GROUP = X * ZL
DOT = dict(preferred_element_type=jnp.float32)
BF, F32 = jnp.bfloat16, jnp.float32
VMEM = pl.BlockSpec(memory_space=pltpu.VMEM)
ANY = pl.BlockSpec(memory_space=pl.ANY)
LIMIT = 24 * 1024 * 1024
FLIPS = (1, 2, 3)


def cost(flops, moved):
    return pl.CostEstimate(flops=flops, bytes_accessed=moved, transcendentals=0)


def spot_of():
    index = lax.axis_index("x")
    for name, size in (("yh", YH), ("zh", ZH), ("zl", ZL)):
        index = index * size + lax.axis_index(name)
    return index


def encode_kernel(sources, weight, bias, dec, latent, mine, src, wts, shift, sems):
    chunks = wts.shape[0]
    depth = wts.shape[1]
    copies = [pltpu.make_async_copy(sources, src, sems.at[chunks])]
    for i in range(chunks):
        part = weight.at[pl.ds(i * depth, depth), :]
        copies.append(pltpu.make_async_copy(part, wts.at[i], sems.at[i]))
    late = [
        pltpu.make_async_copy(bias, shift, sems.at[chunks + 1]),
        pltpu.make_async_copy(dec.at[lax.axis_index("tgt")], mine, sems.at[chunks + 2]),
    ]
    for copy in copies + late:
        copy.start()
    copies[0].wait()
    total = None
    for i in range(chunks):
        copies[i + 1].wait()
        part = jnp.dot(src[:, pl.ds(i * depth, depth)], wts[i], **DOT)
        total = part if total is None else total + part
    late[0].wait()
    latent[...] = jnp.maximum(total + shift[...], 0.0).astype(BF)
    late[1].wait()


def load_kernel(mask, latent, mine, dec, held, own, keep, flags, sems):
    owner = lax.axis_index("tgt")
    first = pltpu.make_async_copy(mask, flags, sems.at[0])
    first.start()
    copies = []
    for flip in FLIPS:
        peer = owner ^ flip
        copies.append(
            pltpu.make_async_copy(dec.at[peer], held.at[flip - 1], sems.at[flip])
        )
    for copy in copies:
        copy.start()
    first.wait()
    for flip in range(TG):
        value = flags[owner, owner ^ flip].astype(F32)
        keep[flip] = jnp.full(keep.shape[1:], value, F32)
    rows = latent[...] * keep[0, 0:1, :].astype(BF)
    own[...] = jnp.dot(rows, mine[...], **DOT)
    for copy in copies:
        copy.wait()


def decode_pair_kernel(keep, own, l1, l2, targets, dec, out):
    base = spot_of() * targets.shape[0]
    tok, width = out.shape
    step = 256
    rows = []
    for flip, ref in ((1, l1), (2, l2)):
        rows.append((flip - 1, ref[...] * keep[flip, 0:1, :].astype(BF)))
    row_ids = lax.broadcasted_iota(jnp.int32, (tok, 1), 0)
    for start in range(0, width, step):
        cols = pl.ds(start, step)
        total = own[:, cols]
        for slab, latent in rows:
            total = total + jnp.dot(latent, dec[slab, :, cols], **DOT)
        for r in range(targets.shape[0]):
            line = targets[r : r + 1, cols].astype(F32)
            total = total - jnp.where(row_ids == base + r, line, 0.0)
        out[:, cols] = total


def decode_last_kernel(keep, most, l3, dec, out):
    step = 256
    latent = l3[...] * keep[3, 0:1, :].astype(BF)
    for start in range(0, out.shape[1], step):
        cols = pl.ds(start, step)
        total = most[:, cols] + jnp.dot(latent, dec[2, :, cols], **DOT)
        out[:, cols] = total.astype(BF)


def gather_sum_kernel(shares, out):
    total = shares[0].astype(F32)
    for i in range(1, shares.shape[0]):
        total = total + shares[i].astype(F32)
    out[...] = total.astype(out.dtype)


def pair_kernel(a, b, out):
    out[...] = (a[...].astype(F32) + b[...].astype(F32)).astype(out.dtype)


def spread_kernel(s0, s1, s2, s3, out):
    total = (s0[...].astype(F32) + s1[...].astype(F32)) + (
        s2[...].astype(F32) + s3[...].astype(F32)
    )
    err = total.astype(BF)
    for i in range(out.shape[0]):
        out[i] = err


def join_kernel(a, b, out):
    out[...] = (a[...] + b[...].astype(F32)).astype(out.dtype)


def turn_kernel(mine, dec, out):
    out[0] = mine[...].T
    for flip in FLIPS:
        out[flip] = dec[flip - 1].T


def term_kernel(flip, keep, err, turned, out):
    term = jnp.dot(err[...], turned[flip], **DOT)
    out[...] = (keep[flip, 0:1, :] * term).astype(out.dtype)


def pick_kernel(err, out):
    base = spot_of() * out.shape[0]
    block = pl.multiple_of(base // 16 * 16, 16)
    value = err[pl.ds(block, 16), :].astype(F32)
    row_ids = lax.broadcasted_iota(jnp.int32, (16, 1), 0) + block
    for r in range(out.shape[0]):
        row = jnp.sum(jnp.where(row_ids == base + r, value, 0.0), axis=0, keepdims=True)
        out[r : r + 1, :] = row.astype(out.dtype)


def swap(value, name, flip):
    size = lax.axis_size(name)
    return lax.ppermute(value, name, [(i, i ^ flip) for i in range(size)])


def in_hbm(value):
    return pltpu.with_memory_space_constraint(value, pltpu.HBM)


def call(kernel, outs, specs, flops=0, moved=0, scratch=(), out_spec=VMEM):
    return pl.pallas_call(
        kernel,
        out_shape=outs,
        in_specs=specs,
        out_specs=out_spec,
        scratch_shapes=scratch,
        cost_estimate=cost(flops, moved),
        compiler_params=pltpu.CompilerParams(vmem_limit_bytes=LIMIT),
    )


def per_device(sources, targets, enc_weight, enc_bias, dec_weight, pair_mask):
    tok, width = sources.shape[1], sources.shape[2]
    feats = enc_weight.shape[2]
    rows_local = targets.shape[1]
    rows = tok // GROUP
    shape = jax.ShapeDtypeStruct

    chunks = 3
    slabs = in_hbm(dec_weight[0])
    latent, mine = call(
        encode_kernel,
        [shape((tok, feats), BF), shape((feats, width), BF)],
        [ANY] * 4,
        2 * tok * feats * width,
        2 * feats * width,
        scratch=[
            pltpu.VMEM((tok, width), BF),
            pltpu.VMEM((chunks, width // chunks, feats), BF),
            pltpu.VMEM((1, feats), F32),
            pltpu.SemaphoreType.DMA((chunks + 3,)),
        ],
        out_spec=[VMEM] * 2,
    )(in_hbm(sources[0]), in_hbm(enc_weight[0]), in_hbm(enc_bias), slabs)
    l2 = swap(latent, "tgt", 2)
    l1 = swap(latent, "tgt", 1)
    flops = 2 * tok * feats * width
    load = call(
        load_kernel,
        [
            shape((TG - 1, feats, width), BF),
            shape((tok, width), F32),
            shape((TG, 8, feats), F32),
        ],
        [ANY, VMEM, VMEM, ANY],
        flops,
        2 * TG * feats * width,
        scratch=[pltpu.SMEM((TG, TG), jnp.int32), pltpu.SemaphoreType.DMA((TG,))],
        out_spec=[VMEM] * 3,
    )
    dec, own, keep = load(in_hbm(pair_mask), latent, mine, slabs)
    l3 = swap(l2, "tgt", 1)
    most = call(decode_pair_kernel, shape((tok, width), F32), [VMEM] * 6, 2 * flops)(
        keep, own, l1, l2, targets[0], dec
    )
    shares = call(decode_last_kernel, shape((tok, width), BF), [VMEM] * 4, flops)(
        keep, most, l3, dec
    )

    shares = shares.reshape(GROUP, rows, width)
    shares = lax.all_to_all(shares, NEAR, 0, 0, tiled=True)
    near = call(gather_sum_kernel, shape((rows, width), BF), [VMEM])(shares)
    other = swap(near, "yh", 1)
    near = call(pair_kernel, shape((rows, width), BF), [VMEM] * 2)(near, other)
    parts = [near] * ZH
    for flip in (2, 3, 1):
        parts[flip] = swap(near, "zh", flip)
    turned = call(turn_kernel, shape((TG, width, feats), BF), [VMEM] * 2)(mine, dec)
    copies = call(spread_kernel, shape((GROUP, rows, width), BF), [VMEM] * 4)(*parts)
    err_full = lax.all_to_all(copies, NEAR, 0, 0, tiled=True).reshape(tok, width)

    def term(flip, kind):
        kernel = functools.partial(term_kernel, flip)
        return call(kernel, shape((tok, feats), kind), [VMEM] * 3, flops)(
            keep, err_full, turned
        )

    diag = term(3, BF)
    diag = swap(diag, "tgt", 1)
    far = term(2, F32)
    far = call(join_kernel, shape((tok, feats), BF), [VMEM] * 2)(far, diag)
    far = swap(far, "tgt", 2)
    near = term(1, BF)
    near = swap(near, "tgt", 1)
    grad = term(0, F32)
    err_local = call(pick_kernel, shape((rows_local, width), BF), [VMEM])(err_full)
    grad = grad + near.astype(F32) + far.astype(F32)
    return (err_local[None], grad.astype(BF)[None])


def solution(mesh):
    grid = Mesh(
        mesh.devices.reshape(X, YH, ZH, ZL, TG), ("x", "yh", "zh", "zl", "tgt")
    )
    in_specs = (
        P("tgt", None, None),
        P("tgt", FEAT, None),
        P("tgt", None, FEAT),
        P("tgt", FEAT),
        P("tgt", None, FEAT, None),
        P(),
    )
    out_specs = (P("tgt", FEAT, None), P("tgt", None, FEAT))
    return jax.shard_map(
        per_device, mesh=grid, in_specs=in_specs, out_specs=out_specs, check_vma=False
    )
```
